128 devices in a mesh: cache: 32 (over x, y, z_lo), batch: 4 (over z_hi, core).
Axes of the slice: x: 4, y: 4, z: 4 (z_hi: 2, z_lo: 2; z = z_hi * 2 + z_lo), core: 2. Of those that a mesh axis runs over, the one named last changes fastest.
Arguments:
- queries: bfloat16 [3, 4096, 768], P(None, 'batch')
- positives: int32 [3, 4096], P(None, 'batch'), may hold values from 0 to 511
- block_list: int32 [3, 32, 192], P(None, 'batch'), may hold values from 0 to 255
- block_count: int32 [3, 32], P(None, 'batch'), may hold values from 1 to 192
- refresh_owner: int32 [3], replicated, may hold values from 0 to 31, as said below
- cache: float32 [32768, 768], P('cache'), may hold values from -6 to 6
- fresh: float32 [16384, 768], P('cache')
Outputs:
- query_grad: float32 [3, 4096, 768], P(None, ('batch', 'cache'))
- cache_grad: float32 [32768, 768], P('cache')
The draws below stay inside these ranges and needn't reach their ends.
Inputs may be any that keep to these rules, and one draw needn't show every extreme that they name: `refresh_owner`: 3 different owners; owner 0 and owner 32 - 1 are always among them.
All inputs are finite; a program needn't handle non-finite values.
Results may differ from the reference program's by a relative error of at most 0.0003.
Values sent between devices are 32-bit elements; how exact they have to be, the bound alone decides.
A program may use at most 128 MiB of HBM per device.

```python
import math
import jax
import jax.numpy as jnp
from jax import lax

D = 768
BLK = 128
CACHE_DEV = 1024
STEPS = 3
SLAB = 512
OWNERS = 32
QUERIES = 4096
QUERY_BLOCKS = 32
BLOCKS = 256
MAXL = 192
N_CACHE = 32


def owner_order(key):
    base_key = jax.random.fold_in(key, 5)
    first_key, second_key = jax.random.split(base_key)
    middle = 1 + jax.random.permutation(first_key, OWNERS - 2)[:STEPS - 2].astype(jnp.int32)
    chosen = jnp.concatenate([jnp.array([0, OWNERS - 1], jnp.int32), middle], axis=0)
    order = jax.random.permutation(second_key, STEPS)
    return jnp.take(chosen, order, axis=0).astype(jnp.int32)


def fresh_values(key):
    base_key = jax.random.fold_in(key, 11)
    return jax.random.normal(base_key, (SLAB * OWNERS, D), jnp.float32)


def draw_refresh_owner(key, part):
    return owner_order(key)


def draw_fresh(key, part):
    return fresh_values(key)


def draw_queries(key, part):
    own_key = jax.random.fold_in(key, 17)
    return jax.random.normal(own_key, (STEPS, QUERIES, D), jnp.float32).astype(jnp.bfloat16)


def draw_block_count(key, part):
    count_key = jax.random.fold_in(key, 23)
    first_key, second_key, third_key = jax.random.split(count_key, 3)
    total = STEPS * QUERY_BLOCKS
    counts = jax.random.randint(first_key, (total,), 1, MAXL + 1, jnp.int32)
    high_slot = jax.random.randint(second_key, (), 0, total, jnp.int32)
    low_slot = (high_slot + 1 + jax.random.randint(third_key, (), 0, total - 1, jnp.int32)) % total
    counts = counts.at[high_slot].set(MAXL).at[low_slot].set(1)
    return counts.reshape(STEPS, QUERY_BLOCKS)


def touch_ends(values, key, smallest, top_value):
    extent = values.shape
    place = [jax.random.randint(jax.random.fold_in(key, axis), (), 0, extent[axis]) for axis in range(len(extent))]
    values = values.at[tuple(place)].set(smallest)
    longest = extent.index(max(extent))
    place[longest] = (place[longest] + 1) % extent[longest]
    return values.at[tuple(place)].set(top_value)


def block_levels(key, dims, cuts, low, top_value):
    factor_of = 1.0
    for position, blocks in cuts:
        heights = jax.random.uniform(jax.random.fold_in(jax.random.fold_in(key, 6), position), (blocks,), jnp.float32, low / len(cuts), top_value / len(cuts))
        factor_of = factor_of * jnp.repeat(jnp.exp(heights), dims[position] // blocks).reshape((-1,) + (1,) * (len(dims) - 1 - position))
    return factor_of


def centred(stream_key, extent, deviation, most, pieces=(), kind=jnp.bfloat16):
    values = deviation * jax.random.normal(stream_key, extent, jnp.float32)
    if pieces:
        values = values * block_levels(stream_key, extent, pieces, -0.22, 0.18)
    return jnp.clip(values, -most, most).astype(kind)


def setup_inputs(seed: int = 0) -> dict:
    streams_of = jax.random.split(jax.random.key(seed), 8)
    queries = draw_queries(jax.random.fold_in(streams_of[7], 71), 0)
    positives = touch_ends(jax.random.randint(streams_of[1], (STEPS, QUERIES), 0, SLAB), jax.random.fold_in(streams_of[1], 1), 0, SLAB - 1).astype(jnp.int32)
    block_list = touch_ends(jax.random.randint(streams_of[2], (STEPS, QUERY_BLOCKS, MAXL), 0, BLOCKS), jax.random.fold_in(streams_of[2], 1), 0, BLOCKS - 1).astype(jnp.int32)
    block_count = draw_block_count(jax.random.fold_in(streams_of[7], 71), 0)
    refresh_owner = draw_refresh_owner(jax.random.fold_in(streams_of[7], 71), 0)
    cache = centred(streams_of[5], (CACHE_DEV * N_CACHE, D), 1.0, 6.0, ((0, 32),), jnp.float32)
    fresh = draw_fresh(jax.random.fold_in(streams_of[7], 71), 0)
    return dict(queries=queries, positives=positives, block_list=block_list, block_count=block_count, refresh_owner=refresh_owner, cache=cache, fresh=fresh)


def reference(queries, positives, block_list, block_count, refresh_owner, cache, fresh):
    scale = 2.0 / math.sqrt(D)
    highest = lax.Precision.HIGHEST
    current = cache
    grad_cache = jnp.zeros(cache.shape, jnp.float32)
    results = []
    block_ids = jnp.arange(BLOCKS, dtype=jnp.int32)
    for step in range(STEPS):
        owner = refresh_owner[step].astype(jnp.int32)
        slab = lax.dynamic_slice_in_dim(fresh, owner * SLAB, SLAB, 0)
        current = lax.dynamic_update_slice_in_dim(current, slab, owner * CACHE_DEV, 0)
        valid = jnp.arange(MAXL, dtype=jnp.int32)[None, :] < block_count[step][:, None]
        hits = (block_list[step][:, :, None] == block_ids[None, None, :]) & valid[:, :, None]
        member = jnp.any(hits, axis=1)
        query_rows = queries[step].astype(jnp.float32).reshape(QUERY_BLOCKS, BLK, D)
        pos_rows = positives[step].reshape(QUERY_BLOCKS, BLK)

        def per_block(carry, item):
            block_q, block_member, block_pos = item
            mask = jnp.repeat(block_member, BLK)
            scores = scale * jnp.dot(block_q, current.T, precision=highest)
            scores = jnp.where(mask[None, :], scores, -1e+30)
            slab_scores = scale * jnp.dot(block_q, slab.T, precision=highest)
            top = jnp.maximum(lax.optimization_barrier(jnp.max(scores, axis=1)), lax.optimization_barrier(jnp.max(slab_scores, axis=1)))
            total = lax.optimization_barrier(jnp.sum(jnp.where(mask[None, :], jnp.exp(scores - top[:, None]), 0.0), axis=1))
            total = total + lax.optimization_barrier(jnp.sum(jnp.exp(slab_scores - top[:, None]), axis=1))
            lse = top + jnp.log(total)
            probs = jnp.where(mask[None, :], jnp.exp(scores - lse[:, None]), 0.0)
            slab_probs = jnp.exp(slab_scores - lse[:, None])
            grad_q = jnp.dot(probs, current, precision=highest) + jnp.dot(slab_probs, slab, precision=highest)
            grad_q = grad_q - jnp.take(slab, block_pos, axis=0)
            carry = carry + jnp.dot(probs.T, block_q, precision=highest)
            return (carry, grad_q)
        grad_cache, grads = lax.scan(per_block, grad_cache, (query_rows, member, pos_rows))
        results.append(grads.reshape(QUERIES, D))
    return (jnp.stack(results, axis=0), grad_cache)
```

```python
import functools
import math

import jax
import jax.numpy as jnp
from jax import lax
from jax.experimental import pallas as pl
from jax.experimental.pallas import tpu as pltpu
from jax.sharding import PartitionSpec as P

BLK = 128
RING = 4
NEG = -1e30
F32 = jnp.float32
BF16 = jnp.bfloat16
NT = (((1,), (1,)), ((), ()))
TN = (((0,), (0,)), ((), ()))
NN = (((1,), (0,)), ((), ()))
ORDER = (2, 1, 3, 0)


def mm(a, b, dims):
    return lax.dot_general(a, b, dims, preferred_element_type=F32)


def halves(x):
    high = x.astype(BF16)
    return high, (x - high.astype(F32)).astype(BF16)


def kernel(
    q_hbm, pos_ref, list_ref, count_ref, owner_ref, cache_hbm, fresh_hbm,
    qg_hbm, cg_hbm,
    q, chi, clo, e, zs, ah, al, mloc, keep, factor, factor_w, posx, lse,
    stat_out, stat_in, t, r1, u, r2, r3, g, pair_in, far_in,
    in_sem, out_sem, send_sem, recv_sem,
):
    steps = q.shape[0]
    rows = q.shape[1] // RING
    width = q.shape[2]
    cols = chi.shape[1]
    blocks = cols // BLK
    slab = fresh_hbm.shape[0]
    slab_blocks = slab // BLK
    quarter = rows // RING
    part = quarter // 2
    half = rows // 2
    list_width = list_ref.shape[2]
    scale = 2.0 / math.sqrt(width)
    log2e = math.log2(math.e)

    ci = lax.axis_index("cache")
    bi = lax.axis_index("batch")
    x, y, zl = ci // 8, (ci // 2) % 4, ci % 2
    zh, core = bi // 2, bi % 2
    one, two = 1 - core, core
    own_a = x * one + y * two
    own_b = y * one + x * two

    def first(d):
        return (((x + d * one) % 4) * 8 + ((y + d * two) % 4) * 2 + zl, bi)

    def second(d):
        return (((x + d * two) % 4) * 8 + ((y + d * one) % 4) * 2 + zl, bi)

    z_peer = (ci + 1 - 2 * zl, bi)
    far_peer = (ci, (1 - zh) * 2 + core)
    pair_peer = (ci, zh * 2 + 1 - core)
    peers = [first(1), first(2), first(3), second(1), second(2), second(3), z_peer, far_peer, pair_peer]

    def remote(number, src, dst, device):
        return pltpu.make_async_remote_copy(
            src_ref=src, dst_ref=dst, send_sem=send_sem.at[number], recv_sem=recv_sem.at[number],
            device_id=device, device_id_type=pl.DeviceIdType.MESH,
        )

    barrier = pltpu.get_barrier_semaphore()
    for peer in peers:
        pl.semaphore_signal(barrier, inc=1, device_id=peer, device_id_type=pl.DeviceIdType.MESH)

    load_c = pltpu.make_async_copy(cache_hbm, g, in_sem.at[0])
    load_c.start()
    loads_f = []
    for i in range(slab // rows):
        loads_f.append(pltpu.make_async_copy(fresh_hbm.at[pl.ds(i * rows, rows)], u.at[i], in_sem.at[1 + i]))
        loads_f[-1].start()
    q_sem = 1 + slab // rows
    for s in range(steps):
        @pl.loop(0, RING * RING)
        def _(i, s=s):
            a, b = i // RING, i % RING
            src = (a * one + b * two) * rows + (b * one + a * two) * quarter
            pltpu.make_async_copy(
                q_hbm.at[s, pl.ds(pl.multiple_of(src, quarter), quarter)],
                q.at[s, pl.ds(pl.multiple_of(i * quarter, quarter), quarter)],
                in_sem.at[q_sem + s],
            ).start()

    lanes = lax.broadcasted_iota(jnp.int32, (blocks, rows), 1)
    slot = lax.broadcasted_iota(jnp.int32, (1, list_width), 1)
    ids = ci * blocks + lax.broadcasted_iota(jnp.int32, (blocks, 1), 0)
    low_lanes = lax.broadcasted_iota(jnp.int32, (8, BLK), 1) < quarter

    def tables(s):
        @pl.loop(0, RING)
        def _(a):
            c = s * RING + a
            listed = jnp.zeros((blocks, rows), F32)
            picked = []
            for b in range(RING):
                block = (2 * a + b // 2) * one + (2 * b + a // 2) * two
                row = list_ref[s, pl.ds(block, 1), :]
                valid = slot < count_ref[s, block]
                hit = jnp.where((row == ids) & valid, 1.0, 0.0)
                hit = jnp.max(hit, axis=1, keepdims=True)
                listed = jnp.where(lanes // quarter == b, hit, listed)
                tile = (2 * a + b // 2) * one + (2 * b + a // 2) * two
                found = pos_ref[pl.ds(s, 1), pl.ds(pl.multiple_of(tile * BLK, BLK), BLK)]
                found = jnp.broadcast_to(found, (8, BLK))
                side = (b % 2) * one + (a % 2) * two
                flag = jnp.broadcast_to(side, (8, BLK)) == b % 2
                picked.append(jnp.where(flag, found, pltpu.roll(found, quarter, 1)))
            keep[c] = listed
            mine = jnp.broadcast_to(owner_ref[s], (8, BLK)) == ci
            for i in range(2):
                both = jnp.where(low_lanes, picked[2 * i], picked[2 * i + 1])
                posx[c, :, i * BLK:(i + 1) * BLK] = jnp.where(mine, both, -1)

    def weights(s, c):
        mine = jnp.broadcast_to(owner_ref[s], (blocks, rows)) == ci
        top = lax.broadcasted_iota(jnp.int32, (blocks, rows), 0) < slab_blocks
        return keep[c] + jnp.where(mine & top, 1.0, 0.0)

    def prepare():
        @pl.loop(0, cols // BLK)
        def _(i):
            at = pl.ds(pl.multiple_of(i * BLK, BLK), BLK)
            high, low = halves(g[at, :])
            for s in range(steps):
                chi[s, at, :] = high
                clo[s, at, :] = low

        @pl.loop(0, slab // BLK)
        def _(i):
            at = pl.ds(pl.multiple_of(i * BLK, BLK), BLK)
            per = rows // BLK
            old = g[at, :]
            new = u[i // per, pl.ds(pl.multiple_of((i % per) * BLK, BLK), BLK), :]
            done = jnp.zeros((BLK, width), jnp.bool_)
            for s in range(steps):
                done = done | (jnp.broadcast_to(owner_ref[s], (BLK, width)) == ci)
                high, low = halves(jnp.where(done, new, old))
                chi[s, at, :] = high
                clo[s, at, :] = low

    def scores(s, begin, count):
        @pl.loop(begin, begin + count)
        def _(a):
            c = s * RING + a
            block_q = q[s, pl.ds(pl.multiple_of(a * rows, rows), rows), :]
            zs[...] = mm(chi[s], block_q, NT) + mm(clo[s], block_q, NT)
            sums = []
            for j in range(blocks):
                at = slice(j * BLK, (j + 1) * BLK)
                z = zs[at, :]
                peak = jnp.max(z, axis=0, keepdims=True)
                value = jnp.exp2((z - peak) * (scale * log2e))
                e[c, at, :] = value
                mloc[c, j:j + 1, :] = peak * scale
                sums.append(jnp.sum(value, axis=0, keepdims=True))
            w = weights(s, c)
            peaks = jnp.where(w > 0.0, mloc[c], NEG)
            top = jnp.max(peaks, axis=0, keepdims=True)
            total = jnp.concatenate(sums, axis=0) * jnp.exp(peaks - top)
            total = jnp.sum(jnp.where(w > 0.0, w * total, 0.0), axis=0, keepdims=True)
            stat_out[s, 0, pl.ds(a, 1), :] = top
            stat_out[s, 0, pl.ds(RING + a, 1), :] = total

    def stat_copy(s, stage):
        base = s * 7 + stage * 3
        if stage == 2:
            return [remote(base, stat_out.at[s, 2], stat_in.at[s, 2, 0], z_peer)]
        where = first if stage == 0 else second
        return [remote(base + d - 1, stat_out.at[s, stage], stat_in.at[s, stage, d - 1], where(d)) for d in (1, 2, 3)]

    sent = []

    def stat_send(s, stage):
        for copy in stat_copy(s, stage):
            copy.start()
            sent.append(copy)

    def stat_merge(s, stage):
        copies = stat_copy(s, stage)
        for copy in copies:
            copy.wait_recv()
        got = [stat_out[s, stage]] + [stat_in[s, stage, i] for i in range(len(copies))]
        tops = [v[:RING] for v in got]
        top = functools.reduce(jnp.maximum, tops)
        total = sum(v[RING:] * jnp.exp(p - top) for v, p in zip(got, tops))
        if stage < 2:
            stat_out[s, stage + 1, :RING, :] = top
            stat_out[s, stage + 1, RING:, :] = total
            stat_send(s, stage + 1)
            return
        lse[s, :RING, :] = top + jnp.log(total)
        for a in range(RING):
            c = s * RING + a
            scaled = jnp.exp(mloc[c] - lse[s, a:a + 1, :])
            w = weights(s, c)
            factor[c] = jnp.where(keep[c] > 0.0, scaled, 0.0)
            factor_w[c] = jnp.where(w > 0.0, w * scaled, 0.0)

    def ring1(s, i):
        right, left = first(1), first(3)
        low, high = pl.ds(0, half), pl.ds(half, half)
        src, device = [
            (t.at[s, 0, low], right), (t.at[s, 0, high], left),
            (t.at[s, 1, high], right), (t.at[s, 1, low], right),
            (t.at[s, 2, low], left), (t.at[s, 2, high], left),
        ][i]
        return remote(21 + s * 13 + i, src, r1.at[s, i], device)

    def start(copy):
        copy.start()
        sent.append(copy)

    def terms(s):
        @pl.loop(0, RING)
        def _(k):
            hop = jnp.where(k == 0, 2, jnp.where(k == 1, 1, jnp.where(k == 2, 3, 0)))
            a = (own_a + hop) % RING
            c = s * RING + a
            place = posx[c, 0:1, :]
            for j in range(blocks):
                at = slice(j * BLK, (j + 1) * BLK)
                value = e[c, at, :] * factor_w[c, j:j + 1, :]
                if j < slab_blocks:
                    row = lax.broadcasted_iota(jnp.int32, (BLK, rows), 0) + j * BLK
                    value = value - jnp.where(row == place, 1.0, 0.0)
                ah[at, :], al[at, :] = halves(value)
            t[s, k] = mm(ah[...], chi[s], TN) + mm(ah[...], clo[s], TN) + mm(al[...], chi[s], TN)

            @pl.when(k == 0)
            def _():
                ring1(s, 0).start()
                ring1(s, 1).start()

            @pl.when(k == 1)
            def _():
                ring1(s, 2).start()

            @pl.when(k == 2)
            def _():
                ring1(s, 4).start()

        sent.extend(ring1(s, i) for i in (0, 1, 2, 4))

    def relay1(s):
        ring1(s, 0).wait_recv()
        t[s, 1, :half, :] += r1[s, 0]
        start(ring1(s, 3))
        ring1(s, 1).wait_recv()
        t[s, 2, half:, :] += r1[s, 1]
        start(ring1(s, 5))

    def piece(s, d, side):
        at = ((own_b + d) % RING) * quarter + side * part
        return u.at[s, pl.ds(pl.multiple_of(at, part), part)]

    def ring2(s, i):
        right, left = second(1), second(3)
        d, side, device = [(2, 0, right), (2, 1, left), (1, 1, right), (1, 0, right), (3, 0, left), (3, 1, left)][i]
        return remote(21 + s * 13 + 6 + i, piece(s, d, side), r2.at[s, i], device)

    def finish1(s):
        for i in (2, 3, 4, 5):
            ring1(s, i).wait_recv()
        u[s, :half, :] = t[s, 3, :half, :] + r1[s, 3] + r1[s, 4]
        u[s, half:, :] = t[s, 3, half:, :] + r1[s, 2] + r1[s, 5]
        for i in (0, 1, 2, 4):
            start(ring2(s, i))

    def relay2(s):
        ring2(s, 0).wait_recv()
        ref = piece(s, 1, 0)
        ref[...] += r2[s, 0]
        start(ring2(s, 3))
        ring2(s, 1).wait_recv()
        ref = piece(s, 3, 1)
        ref[...] += r2[s, 1]
        start(ring2(s, 5))

    def last(s):
        return remote(21 + s * 13 + 12, piece(s, 0, 1 - zl), r3.at[s], z_peer)

    def finish2(s):
        for i in (2, 3, 4, 5):
            ring2(s, i).wait_recv()
        ref = piece(s, 0, 0)
        ref[...] += r2[s, 3] + r2[s, 4]
        ref = piece(s, 0, 1)
        ref[...] += r2[s, 2] + r2[s, 5]
        start(last(s))

    def finish3(s):
        last(s).wait_recv()
        ref = piece(s, 0, zl)
        ref[...] += r3[s]
        out_copy(s).start()

    def out_copy(s):
        return pltpu.make_async_copy(piece(s, 0, zl), qg_hbm.at[s], out_sem.at[s])

    side_rows = cols // 2
    other_at = pl.ds(pl.multiple_of((1 - core) * side_rows, side_rows), side_rows)
    mine_at = pl.ds(pl.multiple_of(core * side_rows, side_rows), side_rows)
    base = 21 + steps * 13
    pair_copy = remote(base, g.at[other_at], pair_in, pair_peer)
    far_copy = remote(base + 1, g.at[mine_at], far_in, far_peer)
    final_copy = remote(base + 2, g.at[mine_at], cg_hbm.at[mine_at], pair_peer)
    final_local = pltpu.make_async_copy(g.at[mine_at], cg_hbm.at[mine_at], out_sem.at[steps])

    def gradient(side, at):
        g[at, :] = jnp.zeros((side_rows, width), F32)

        @pl.loop(0, steps * RING)
        def _(c):
            s, a = c // RING, c % RING
            for j in range(side_rows // BLK):
                where = pl.ds(pl.multiple_of(side * side_rows, side_rows) + j * BLK, BLK)
                scaled = factor[c, pl.ds(side * (side_rows // BLK) + j, 1), :]
                put = slice(j * BLK, (j + 1) * BLK)
                ah[put, :], al[put, :] = halves(e[c, where, :] * scaled)
            block_q = q[s, pl.ds(pl.multiple_of(a * rows, rows), rows), :]
            g[at, :] += mm(ah[:side_rows, :], block_q, NN) + mm(al[:side_rows, :], block_q, NN)

    load_c.wait()
    for load in loads_f:
        load.wait()
    prepare()
    for s in range(steps):
        tables(s)

    def q_ready(s):
        pltpu.make_async_copy(q_hbm.at[s], q.at[s], in_sem.at[q_sem + s]).wait()

    q_ready(0)
    scores(0, 0, RING)
    pl.semaphore_wait(barrier, len(peers))
    stat_send(0, 0)
    q_ready(1)
    scores(1, 0, 2)
    stat_merge(0, 0)
    scores(1, 2, 2)
    stat_merge(0, 1)
    stat_send(1, 0)
    q_ready(2)
    scores(2, 0, 1)
    stat_merge(0, 2)
    terms(0)
    stat_merge(1, 0)
    scores(2, 1, 1)
    stat_merge(1, 1)
    relay1(0)
    scores(2, 2, 2)
    stat_send(2, 0)
    stat_merge(1, 2)
    terms(1)
    stat_merge(2, 0)
    finish1(0)
    relay1(1)
    stat_merge(2, 1)
    relay2(0)
    stat_merge(2, 2)
    gradient(1 - core, other_at)
    pair_copy.start()
    terms(2)
    finish2(0)
    finish1(1)
    relay1(2)
    finish3(0)
    relay2(1)
    gradient(core, mine_at)
    pair_copy.wait_recv()
    g[mine_at, :] += pair_in[...]
    far_copy.start()
    finish2(1)
    finish1(2)
    finish3(1)
    relay2(2)
    finish2(2)
    finish3(2)
    far_copy.wait()
    g[mine_at, :] += far_in[...]
    final_copy.start()
    final_local.start()
    for copy in sent:
        copy.wait_send()
    pair_copy.wait_send()
    for s in range(steps):
        out_copy(s).wait()
    final_local.wait()
    final_copy.wait()


def on_device(queries, positives, block_list, block_count, refresh_owner, cache, fresh):
    steps, group_rows, width = queries.shape
    cols = cache.shape[0]
    owners = lax.axis_size("cache")
    share = group_rows // owners
    rows = group_rows // RING
    chunks = steps * RING
    blocks = cols // BLK
    half, part = rows // 2, rows // RING // 2
    messages = 21 + steps * 13 + 3
    vmem = pl.BlockSpec(memory_space=pltpu.VMEM)
    smem = pl.BlockSpec(memory_space=pltpu.SMEM)
    anywhere = pl.BlockSpec(memory_space=pl.ANY)
    small = pltpu.VMEM((chunks, blocks, rows), F32)
    return pl.pallas_call(
        kernel,
        out_shape=(
            jax.ShapeDtypeStruct((steps, share, width), F32),
            jax.ShapeDtypeStruct((cols, width), F32),
        ),
        in_specs=[anywhere, vmem, vmem, smem, smem, anywhere, anywhere],
        out_specs=(anywhere, anywhere),
        scratch_shapes=[
            pltpu.VMEM((steps, group_rows, width), BF16),
            pltpu.VMEM((steps, cols, width), BF16),
            pltpu.VMEM((steps, cols, width), BF16),
            pltpu.VMEM((chunks, cols, rows), F32),
            pltpu.VMEM((cols, rows), F32),
            pltpu.VMEM((cols, rows), BF16),
            pltpu.VMEM((cols, rows), BF16),
            small, small, small, small,
            pltpu.VMEM((chunks, 8, rows), jnp.int32),
            pltpu.VMEM((steps, 8, rows), F32),
            pltpu.VMEM((steps, 3, 8, rows), F32),
            pltpu.VMEM((steps, 3, 3, 8, rows), F32),
            pltpu.VMEM((steps, RING, rows, width), F32),
            pltpu.VMEM((steps, 6, half, width), F32),
            pltpu.VMEM((steps, rows, width), F32),
            pltpu.VMEM((steps, 6, part, width), F32),
            pltpu.VMEM((steps, part, width), F32),
            pltpu.VMEM((cols, width), F32),
            pltpu.VMEM((cols // 2, width), F32),
            pltpu.VMEM((cols // 2, width), F32),
            pltpu.SemaphoreType.DMA((1 + fresh.shape[0] // rows + steps,)),
            pltpu.SemaphoreType.DMA((steps + 1,)),
            pltpu.SemaphoreType.DMA((messages,)),
            pltpu.SemaphoreType.DMA((messages,)),
        ],
        compiler_params=pltpu.CompilerParams(
            collective_id=0, has_side_effects=True, vmem_limit_bytes=67_043_328
        ),
        name="cache_step",
    )(queries, positives, block_list, block_count, refresh_owner, cache, fresh)


def solution(mesh):
    return jax.shard_map(
        on_device,
        mesh=mesh,
        in_specs=(
            P(None, "batch", None),
            P(None, "batch"),
            P(None, "batch", None),
            P(None, "batch"),
            P(),
            P("cache", None),
            P("cache", None),
        ),
        out_specs=(P(None, ("batch", "cache"), None), P("cache", None)),
        check_vma=False,
    )
```

```python
import functools
import math

import jax
import jax.numpy as jnp
from jax import lax
from jax.experimental import pallas as pl
from jax.experimental.pallas import tpu as pltpu
from jax.sharding import PartitionSpec as P

BLK = 128
RING = 4
NEG = -1e30
F32 = jnp.float32
BF16 = jnp.bfloat16
NT = (((1,), (1,)), ((), ()))
TN = (((0,), (0,)), ((), ()))
NN = (((1,), (0,)), ((), ()))
ORDER = (2, 1, 3, 0)


def mm(a, b, dims):
    return lax.dot_general(a, b, dims, preferred_element_type=F32)


def halves(x):
    high = x.astype(BF16)
    return high, (x - high.astype(F32)).astype(BF16)


def kernel(
    q_hbm, pos_ref, list_ref, count_ref, owner_ref, cache_hbm, fresh_hbm,
    qg_hbm, cg_hbm,
    q, chi, clo, e, zs, ah, al, dh, dl, mloc, keep, factor, factor_w, posx, lse,
    stat_out, stat_in, t, r1, u, r2, r3, g, pair_in, far_in,
    in_sem, out_sem, send_sem, recv_sem,
):
    steps = q.shape[0]
    rows = q.shape[1] // RING
    width = q.shape[2]
    cols = chi.shape[1]
    blocks = cols // BLK
    slab = fresh_hbm.shape[0]
    slab_blocks = slab // BLK
    quarter = rows // RING
    part = quarter // 2
    half = rows // 2
    list_width = list_ref.shape[2]
    scale = 2.0 / math.sqrt(width)
    log2e = math.log2(math.e)

    ci = lax.axis_index("cache")
    bi = lax.axis_index("batch")
    x, y, zl = ci // 8, (ci // 2) % 4, ci % 2
    zh, core = bi // 2, bi % 2
    one, two = 1 - core, core
    own_a = x * one + y * two
    own_b = y * one + x * two

    def first(d):
        return (((x + d * one) % 4) * 8 + ((y + d * two) % 4) * 2 + zl, bi)

    def second(d):
        return (((x + d * two) % 4) * 8 + ((y + d * one) % 4) * 2 + zl, bi)

    z_peer = (ci + 1 - 2 * zl, bi)
    far_peer = (ci, (1 - zh) * 2 + core)
    pair_peer = (ci, zh * 2 + 1 - core)
    peers = [first(1), first(2), first(3), second(1), second(2), second(3), z_peer, far_peer, pair_peer]

    def remote(number, src, dst, device):
        return pltpu.make_async_remote_copy(
            src_ref=src, dst_ref=dst, send_sem=send_sem.at[number], recv_sem=recv_sem.at[number],
            device_id=device, device_id_type=pl.DeviceIdType.MESH,
        )

    barrier = pltpu.get_barrier_semaphore()
    for peer in peers:
        pl.semaphore_signal(barrier, inc=1, device_id=peer, device_id_type=pl.DeviceIdType.MESH)

    load_c = pltpu.make_async_copy(cache_hbm, g, in_sem.at[0])
    load_c.start()
    loads_f = []
    for i in range(slab // rows):
        loads_f.append(pltpu.make_async_copy(fresh_hbm.at[pl.ds(i * rows, rows)], u.at[i], in_sem.at[1 + i]))
        loads_f[-1].start()
    q_sem = 1 + slab // rows
    for s in range(steps):
        @pl.loop(0, RING * RING)
        def _(i, s=s):
            a, b = i // RING, i % RING
            src = (a * one + b * two) * rows + (b * one + a * two) * quarter
            pltpu.make_async_copy(
                q_hbm.at[s, pl.ds(pl.multiple_of(src, quarter), quarter)],
                q.at[s, pl.ds(pl.multiple_of(i * quarter, quarter), quarter)],
                in_sem.at[q_sem + s],
            ).start()

    lanes = lax.broadcasted_iota(jnp.int32, (blocks, rows), 1)
    slot = lax.broadcasted_iota(jnp.int32, (1, list_width), 1)
    ids = ci * blocks + lax.broadcasted_iota(jnp.int32, (blocks, 1), 0)
    low_lanes = lax.broadcasted_iota(jnp.int32, (8, BLK), 1) < quarter

    def tables(s):
        @pl.loop(0, RING)
        def _(a):
            c = s * RING + a
            listed = jnp.zeros((blocks, rows), F32)
            picked = []
            for b in range(RING):
                block = (2 * a + b // 2) * one + (2 * b + a // 2) * two
                row = list_ref[s, pl.ds(block, 1), :]
                valid = slot < count_ref[s, block]
                hit = jnp.where((row == ids) & valid, 1.0, 0.0)
                hit = jnp.max(hit, axis=1, keepdims=True)
                listed = jnp.where(lanes // quarter == b, hit, listed)
                tile = (2 * a + b // 2) * one + (2 * b + a // 2) * two
                found = pos_ref[pl.ds(s, 1), pl.ds(pl.multiple_of(tile * BLK, BLK), BLK)]
                found = jnp.broadcast_to(found, (8, BLK))
                side = (b % 2) * one + (a % 2) * two
                flag = jnp.broadcast_to(side, (8, BLK)) == b % 2
                picked.append(jnp.where(flag, found, pltpu.roll(found, quarter, 1)))
            keep[c] = listed
            mine = jnp.broadcast_to(owner_ref[s], (8, BLK)) == ci
            for i in range(2):
                both = jnp.where(low_lanes, picked[2 * i], picked[2 * i + 1])
                posx[c, :, i * BLK:(i + 1) * BLK] = jnp.where(mine, both, -1)

    def weights(s, c):
        mine = jnp.broadcast_to(owner_ref[s], (blocks, rows)) == ci
        top = lax.broadcasted_iota(jnp.int32, (blocks, rows), 0) < slab_blocks
        return keep[c] + jnp.where(mine & top, 1.0, 0.0)

    def prepare():
        @pl.loop(0, cols // BLK)
        def _(i):
            at = pl.ds(pl.multiple_of(i * BLK, BLK), BLK)
            high, low = halves(g[at, :])
            for s in range(steps):
                chi[s, at, :] = high
                clo[s, at, :] = low

        @pl.loop(0, slab // BLK)
        def _(i):
            at = pl.ds(pl.multiple_of(i * BLK, BLK), BLK)
            per = rows // BLK
            old = g[at, :]
            new = u[i // per, pl.ds(pl.multiple_of((i % per) * BLK, BLK), BLK), :]
            done = jnp.zeros((BLK, width), jnp.bool_)
            for s in range(steps):
                done = done | (jnp.broadcast_to(owner_ref[s], (BLK, width)) == ci)
                high, low = halves(jnp.where(done, new, old))
                chi[s, at, :] = high
                clo[s, at, :] = low

    def scores(s, begin, count):
        @pl.loop(begin, begin + count)
        def _(h):
            block_q = q[s, pl.ds(pl.multiple_of(h * 2 * rows, 2 * rows), 2 * rows), :]
            zs[...] = mm(chi[s], block_q, NT) + mm(clo[s], block_q, NT)
            for i in range(2):
                a = 2 * h + i
                c = s * RING + a
                sums = []
                for j in range(blocks):
                    at = slice(j * BLK, (j + 1) * BLK)
                    z = zs[at, i * rows:(i + 1) * rows]
                    peak = jnp.max(z, axis=0, keepdims=True)
                    value = jnp.exp2((z - peak) * (scale * log2e))
                    e[c, at, :] = value
                    mloc[c, j:j + 1, :] = peak * scale
                    sums.append(jnp.sum(value, axis=0, keepdims=True))
                w = weights(s, c)
                peaks = jnp.where(w > 0.0, mloc[c], NEG)
                top = jnp.max(peaks, axis=0, keepdims=True)
                total = jnp.concatenate(sums, axis=0) * jnp.exp(peaks - top)
                total = jnp.sum(jnp.where(w > 0.0, w * total, 0.0), axis=0, keepdims=True)
                stat_out[s, 0, pl.ds(a, 1), :] = top
                stat_out[s, 0, pl.ds(RING + a, 1), :] = total

    def stat_copy(s, stage):
        base = s * 7 + stage * 3
        if stage == 2:
            return [remote(base, stat_out.at[s, 2], stat_in.at[s, 2, 0], z_peer)]
        where = first if stage == 0 else second
        return [remote(base + d - 1, stat_out.at[s, stage], stat_in.at[s, stage, d - 1], where(d)) for d in (1, 2, 3)]

    sent = []

    def stat_send(s, stage):
        for copy in stat_copy(s, stage):
            copy.start()
            sent.append(copy)

    def stat_merge(s, stage):
        copies = stat_copy(s, stage)
        for copy in copies:
            copy.wait_recv()
        got = [stat_out[s, stage]] + [stat_in[s, stage, i] for i in range(len(copies))]
        tops = [v[:RING] for v in got]
        top = functools.reduce(jnp.maximum, tops)
        total = sum(v[RING:] * jnp.exp(p - top) for v, p in zip(got, tops))
        if stage < 2:
            stat_out[s, stage + 1, :RING, :] = top
            stat_out[s, stage + 1, RING:, :] = total
            stat_send(s, stage + 1)
            return
        lse[s, :RING, :] = top + jnp.log(total)
        for a in range(RING):
            c = s * RING + a
            scaled = jnp.exp(mloc[c] - lse[s, a:a + 1, :])
            w = weights(s, c)
            factor[c] = jnp.where(keep[c] > 0.0, scaled, 0.0)
            factor_w[c] = jnp.where(w > 0.0, w * scaled, 0.0)

    def ring1(s, i):
        right, left = first(1), first(3)
        low, high = pl.ds(0, half), pl.ds(half, half)
        src, device = [
            (t.at[s, 0, low], right), (t.at[s, 0, high], left),
            (t.at[s, 1, high], right), (t.at[s, 1, low], right),
            (t.at[s, 2, low], left), (t.at[s, 2, high], left),
        ][i]
        return remote(21 + s * 13 + i, src, r1.at[s, i], device)

    def start(copy):
        copy.start()
        sent.append(copy)

    def terms(s, begin, end):
        @pl.loop(begin, end)
        def _(k):
            hop = jnp.where(k == 0, 2, jnp.where(k == 1, 1, jnp.where(k == 2, 3, 0)))
            a = (own_a + hop) % RING
            c = s * RING + a
            place = posx[c, 0:1, :]
            for j in range(blocks):
                at = slice(j * BLK, (j + 1) * BLK)
                value = e[c, at, :] * factor_w[c, j:j + 1, :]
                if j < slab_blocks:
                    row = lax.broadcasted_iota(jnp.int32, (BLK, rows), 0) + j * BLK
                    value = value - jnp.where(row == place, 1.0, 0.0)
                ah[at, :], al[at, :] = halves(value)
            t[s, k] = mm(ah[...], chi[s], TN) + mm(ah[...], clo[s], TN) + mm(al[...], chi[s], TN)

            @pl.when(k == 0)
            def _():
                ring1(s, 0).start()
                ring1(s, 1).start()

            @pl.when(k == 1)
            def _():
                ring1(s, 2).start()

            @pl.when(k == 2)
            def _():
                ring1(s, 4).start()

        if end == RING:
            sent.extend(ring1(s, i) for i in (0, 1, 2, 4))

    def relay1(s):
        ring1(s, 0).wait_recv()
        t[s, 1, :half, :] += r1[s, 0]
        start(ring1(s, 3))
        ring1(s, 1).wait_recv()
        t[s, 2, half:, :] += r1[s, 1]
        start(ring1(s, 5))

    def piece(s, d, side):
        at = ((own_b + d) % RING) * quarter + side * part
        return u.at[s, pl.ds(pl.multiple_of(at, part), part)]

    def ring2(s, i):
        right, left = second(1), second(3)
        d, side, device = [(2, 0, right), (2, 1, left), (1, 1, right), (1, 0, right), (3, 0, left), (3, 1, left)][i]
        return remote(21 + s * 13 + 6 + i, piece(s, d, side), r2.at[s, i], device)

    def finish1(s):
        for i in (2, 3, 4, 5):
            ring1(s, i).wait_recv()
        u[s, :half, :] = t[s, 3, :half, :] + r1[s, 3] + r1[s, 4]
        u[s, half:, :] = t[s, 3, half:, :] + r1[s, 2] + r1[s, 5]
        for i in (0, 1, 2, 4):
            start(ring2(s, i))

    def relay2(s):
        ring2(s, 0).wait_recv()
        ref = piece(s, 1, 0)
        ref[...] += r2[s, 0]
        start(ring2(s, 3))
        ring2(s, 1).wait_recv()
        ref = piece(s, 3, 1)
        ref[...] += r2[s, 1]
        start(ring2(s, 5))

    def last(s):
        return remote(21 + s * 13 + 12, piece(s, 0, 1 - zl), r3.at[s], z_peer)

    def finish2(s):
        for i in (2, 3, 4, 5):
            ring2(s, i).wait_recv()
        ref = piece(s, 0, 0)
        ref[...] += r2[s, 3] + r2[s, 4]
        ref = piece(s, 0, 1)
        ref[...] += r2[s, 2] + r2[s, 5]
        start(last(s))

    def finish3(s):
        last(s).wait_recv()
        ref = piece(s, 0, zl)
        ref[...] += r3[s]
        out_copy(s).start()

    def out_copy(s):
        return pltpu.make_async_copy(piece(s, 0, zl), qg_hbm.at[s], out_sem.at[s])

    side = cols // 2
    pieces = side // BLK
    base = 21 + steps * 13

    def spot(which, p):
        return pl.ds(pl.multiple_of(which * side + p * BLK, BLK), BLK)

    def pair_copy(p):
        return remote(base + p, g.at[spot(1 - core, p)], pair_in.at[p], pair_peer)

    def far_copy(p):
        return remote(base + pieces + p, g.at[spot(core, p)], far_in.at[p], far_peer)

    def final_copy(p):
        at = spot(core, p)
        return remote(base + 2 * pieces + p, g.at[at], cg_hbm.at[at], pair_peer)

    def final_local(p):
        at = spot(core, p)
        return pltpu.make_async_copy(g.at[at], cg_hbm.at[at], out_sem.at[steps + p])

    def gradient(p):
        for i, which in enumerate((1 - core, core)):
            for c in range(steps * RING):
                scaled = factor[c, pl.ds(which * pieces + p, 1), :]
                put = (slice(i * BLK, (i + 1) * BLK), slice(c * rows, (c + 1) * rows))
                dh[put], dl[put] = halves(e[c, spot(which, p), :] * scaled)
        every = q[...].reshape(steps * RING * rows, width)
        both = mm(dh[...], every, NN) + mm(dl[...], every, NN)
        g[spot(1 - core, p), :] = both[:BLK]
        g[spot(core, p), :] = both[BLK:]
        start(pair_copy(p))

    def pair_add(p):
        pair_copy(p).wait_recv()
        g[spot(core, p), :] += pair_in[p]
        far_copy(p).start()

    def far_add(p):
        far_copy(p).wait()
        g[spot(core, p), :] += far_in[p]
        final_copy(p).start()
        final_local(p).start()

    def q_ready(s):
        pltpu.make_async_copy(q_hbm.at[s], q.at[s], in_sem.at[q_sem + s]).wait()

    for s in range(steps):
        tables(s)
    load_c.wait()
    for load in loads_f:
        load.wait()
    prepare()

    q_ready(0)
    scores(0, 0, 2)
    pl.semaphore_wait(barrier, len(peers))
    stat_send(0, 0)
    q_ready(1)
    scores(1, 0, 1)
    stat_merge(0, 0)
    scores(1, 1, 1)
    stat_send(1, 0)
    stat_merge(0, 1)
    q_ready(2)
    scores(2, 0, 1)
    stat_merge(0, 2)
    stat_merge(1, 0)
    terms(0, 0, 1)
    scores(2, 1, 1)
    stat_send(2, 0)
    stat_merge(1, 1)
    terms(0, 1, 3)
    stat_merge(1, 2)
    stat_merge(2, 0)
    terms(0, 3, 4)
    stat_merge(2, 1)
    relay1(0)
    terms(1, 0, 1)
    stat_merge(2, 2)
    gradient(0)
    terms(1, 1, 2)
    pair_add(0)
    terms(1, 2, 4)
    finish1(0)
    gradient(1)
    relay1(1)
    relay2(0)
    terms(2, 0, 2)
    pair_add(1)
    finish2(0)
    terms(2, 2, 4)
    finish3(0)
    gradient(2)
    finish1(1)
    pair_add(2)
    gradient(3)
    relay1(2)
    relay2(1)
    pair_add(3)
    far_add(0)
    finish2(1)
    far_add(1)
    finish3(1)
    far_add(2)
    finish1(2)
    relay2(2)
    finish2(2)
    finish3(2)
    far_add(3)
    for copy in sent:
        copy.wait_send()
    for s in range(steps):
        out_copy(s).wait()
    for p in range(pieces):
        final_local(p).wait()
        final_copy(p).wait()


def on_device(queries, positives, block_list, block_count, refresh_owner, cache, fresh):
    steps, group_rows, width = queries.shape
    cols = cache.shape[0]
    owners = lax.axis_size("cache")
    share = group_rows // owners
    rows = group_rows // RING
    chunks = steps * RING
    blocks = cols // BLK
    half, part = rows // 2, rows // RING // 2
    pieces = cols // 2 // BLK
    messages = 21 + steps * 13 + 3 * pieces
    vmem = pl.BlockSpec(memory_space=pltpu.VMEM)
    smem = pl.BlockSpec(memory_space=pltpu.SMEM)
    anywhere = pl.BlockSpec(memory_space=pl.ANY)
    small = pltpu.VMEM((chunks, blocks, rows), F32)
    return pl.pallas_call(
        kernel,
        out_shape=(
            jax.ShapeDtypeStruct((steps, share, width), F32),
            jax.ShapeDtypeStruct((cols, width), F32),
        ),
        in_specs=[anywhere, vmem, vmem, smem, smem, anywhere, anywhere],
        out_specs=(anywhere, anywhere),
        scratch_shapes=[
            pltpu.VMEM((steps, group_rows, width), BF16),
            pltpu.VMEM((steps, cols, width), BF16),
            pltpu.VMEM((steps, cols, width), BF16),
            pltpu.VMEM((chunks, cols, rows), F32),
            pltpu.VMEM((cols, 2 * rows), F32),
            pltpu.VMEM((cols, rows), BF16),
            pltpu.VMEM((cols, rows), BF16),
            pltpu.VMEM((2 * BLK, chunks * rows), BF16),
            pltpu.VMEM((2 * BLK, chunks * rows), BF16),
            small, small, small, small,
            pltpu.VMEM((chunks, 8, rows), jnp.int32),
            pltpu.VMEM((steps, 8, rows), F32),
            pltpu.VMEM((steps, 3, 8, rows), F32),
            pltpu.VMEM((steps, 3, 3, 8, rows), F32),
            pltpu.VMEM((steps, RING, rows, width), F32),
            pltpu.VMEM((steps, 6, half, width), F32),
            pltpu.VMEM((steps, rows, width), F32),
            pltpu.VMEM((steps, 6, part, width), F32),
            pltpu.VMEM((steps, part, width), F32),
            pltpu.VMEM((cols, width), F32),
            pltpu.VMEM((pieces, BLK, width), F32),
            pltpu.VMEM((pieces, BLK, width), F32),
            pltpu.SemaphoreType.DMA((1 + fresh.shape[0] // rows + steps,)),
            pltpu.SemaphoreType.DMA((steps + pieces,)),
            pltpu.SemaphoreType.DMA((messages,)),
            pltpu.SemaphoreType.DMA((messages,)),
        ],
        compiler_params=pltpu.CompilerParams(
            collective_id=0, has_side_effects=True, vmem_limit_bytes=67_043_328
        ),
        name="cache_step",
    )(queries, positives, block_list, block_count, refresh_owner, cache, fresh)


def solution(mesh):
    return jax.shard_map(
        on_device,
        mesh=mesh,
        in_specs=(
            P(None, "batch", None),
            P(None, "batch"),
            P(None, "batch", None),
            P(None, "batch"),
            P(),
            P("cache", None),
            P("cache", None),
        ),
        out_specs=(P(None, ("batch", "cache"), None), P("cache", None)),
        check_vma=False,
    )
```

```python
import functools
import math

import jax
import jax.numpy as jnp
from jax import lax
from jax.experimental import pallas as pl
from jax.experimental.pallas import tpu as pltpu
from jax.sharding import PartitionSpec as P

BLK = 128
RING = 4
NEG = -1e30
F32 = jnp.float32
BF16 = jnp.bfloat16
NT = (((1,), (1,)), ((), ()))
TN = (((0,), (0,)), ((), ()))
NN = (((1,), (0,)), ((), ()))
ORDER = (2, 1, 3, 0)


def mm(a, b, dims):
    return lax.dot_general(a, b, dims, preferred_element_type=F32)


def halves(x):
    high = x.astype(BF16)
    return high, (x - high.astype(F32)).astype(BF16)


def kernel(
    q_hbm, pos_ref, list_ref, count_ref, owner_ref, cache_hbm, fresh_hbm,
    qg_hbm, cg_hbm,
    q, chi, clo, e, zs, ah, al, dh, dl, mloc, keep, factor, factor_w, posx, lse,
    stat_out, stat_in, t, r1, u, r2, r3, g, pair_in, far_in,
    in_sem, out_sem, send_sem, recv_sem,
):
    steps = q.shape[0]
    rows = q.shape[1] // RING
    width = q.shape[2]
    cols = chi.shape[1]
    blocks = cols // BLK
    slab = fresh_hbm.shape[0]
    slab_blocks = slab // BLK
    quarter = rows // RING
    part = quarter // 2
    half = rows // 2
    list_width = list_ref.shape[2]
    scale = 2.0 / math.sqrt(width)
    log2e = math.log2(math.e)

    ci = lax.axis_index("cache")
    bi = lax.axis_index("batch")
    x, y, zl = ci // 8, (ci // 2) % 4, ci % 2
    zh, core = bi // 2, bi % 2
    one, two = 1 - core, core
    own_a = x * one + y * two
    own_b = y * one + x * two

    def first(d):
        return (((x + d * one) % 4) * 8 + ((y + d * two) % 4) * 2 + zl, bi)

    def second(d):
        return (((x + d * two) % 4) * 8 + ((y + d * one) % 4) * 2 + zl, bi)

    def flip(device):
        return (device[0] + 1 - 2 * zl, device[1])

    z_peer = flip((ci, bi))
    far_peer = (ci, (1 - zh) * 2 + core)
    pair_peer = (ci, zh * 2 + 1 - core)
    near = [second(1), second(2), second(3), z_peer, flip(second(1)), flip(second(2)), flip(second(3))]
    across = [first(1), first(2), first(3)]
    peers = near + across + [far_peer, pair_peer]

    def remote(number, src, dst, device):
        return pltpu.make_async_remote_copy(
            src_ref=src, dst_ref=dst, send_sem=send_sem.at[number], recv_sem=recv_sem.at[number],
            device_id=device, device_id_type=pl.DeviceIdType.MESH,
        )

    stat_messages = len(near) + len(across)
    base0 = steps * stat_messages
    barrier = pltpu.get_barrier_semaphore()
    for peer in peers:
        pl.semaphore_signal(barrier, inc=1, device_id=peer, device_id_type=pl.DeviceIdType.MESH)

    load_c = pltpu.make_async_copy(cache_hbm, g, in_sem.at[0])
    load_c.start()
    loads_f = []
    for i in range(slab // rows):
        loads_f.append(pltpu.make_async_copy(fresh_hbm.at[pl.ds(i * rows, rows)], u.at[i], in_sem.at[1 + i]))
        loads_f[-1].start()
    q_sem = 1 + slab // rows

    def load_q(s):
        @pl.loop(0, RING * RING)
        def _(i):
            a, b = i // RING, i % RING
            src = (a * one + b * two) * rows + (b * one + a * two) * quarter
            pltpu.make_async_copy(
                q_hbm.at[s, pl.ds(pl.multiple_of(src, quarter), quarter)],
                q.at[s, pl.ds(pl.multiple_of(i * quarter, quarter), quarter)],
                in_sem.at[q_sem + s],
            ).start()

    load_q(0)

    lanes = lax.broadcasted_iota(jnp.int32, (blocks, rows), 1)
    slot = lax.broadcasted_iota(jnp.int32, (1, list_width), 1)
    ids = ci * blocks + lax.broadcasted_iota(jnp.int32, (blocks, 1), 0)
    low_lanes = lax.broadcasted_iota(jnp.int32, (8, BLK), 1) < quarter

    def tables(s):
        @pl.loop(0, RING)
        def _(a):
            c = s * RING + a
            listed = jnp.zeros((blocks, rows), F32)
            picked = []
            for b in range(RING):
                block = (2 * a + b // 2) * one + (2 * b + a // 2) * two
                row = list_ref[s, pl.ds(block, 1), :]
                valid = slot < count_ref[s, block]
                hit = jnp.where((row == ids) & valid, 1.0, 0.0)
                hit = jnp.max(hit, axis=1, keepdims=True)
                listed = jnp.where(lanes // quarter == b, hit, listed)
                tile = (2 * a + b // 2) * one + (2 * b + a // 2) * two
                found = pos_ref[pl.ds(s, 1), pl.ds(pl.multiple_of(tile * BLK, BLK), BLK)]
                found = jnp.broadcast_to(found, (8, BLK))
                side = (b % 2) * one + (a % 2) * two
                flag = jnp.broadcast_to(side, (8, BLK)) == b % 2
                picked.append(jnp.where(flag, found, pltpu.roll(found, quarter, 1)))
            keep[c] = listed
            mine = jnp.broadcast_to(owner_ref[s], (8, BLK)) == ci
            for i in range(2):
                both = jnp.where(low_lanes, picked[2 * i], picked[2 * i + 1])
                posx[c, :, i * BLK:(i + 1) * BLK] = jnp.where(mine, both, -1)

    def weights(s, c):
        mine = jnp.broadcast_to(owner_ref[s], (blocks, rows)) == ci
        top = lax.broadcasted_iota(jnp.int32, (blocks, rows), 0) < slab_blocks
        return keep[c] + jnp.where(mine & top, 1.0, 0.0)

    def prepare(begin, end):
        @pl.loop(slab // BLK, cols // BLK)
        def _(i):
            at = pl.ds(pl.multiple_of(i * BLK, BLK), BLK)
            high, low = halves(g[at, :])
            for s in range(begin, end):
                chi[s, at, :] = high
                clo[s, at, :] = low

        @pl.loop(0, slab // BLK)
        def _(i):
            at = pl.ds(pl.multiple_of(i * BLK, BLK), BLK)
            per = rows // BLK
            old = g[at, :]
            new = u[i // per, pl.ds(pl.multiple_of((i % per) * BLK, BLK), BLK), :]
            done = jnp.zeros((BLK, width), jnp.bool_)
            for s in range(end):
                done = done | (jnp.broadcast_to(owner_ref[s], (BLK, width)) == ci)
                if s >= begin:
                    high, low = halves(jnp.where(done, new, old))
                    chi[s, at, :] = high
                    clo[s, at, :] = low

    def scores(s, h):
        block_q = q[s, pl.ds(pl.multiple_of(h * 2 * rows, 2 * rows), 2 * rows), :]
        zs[...] = mm(chi[s], block_q, NT) + mm(clo[s], block_q, NT)
        for i in range(2):
            a = 2 * h + i
            c = s * RING + a
            sums = []
            for j in range(blocks):
                at = slice(j * BLK, (j + 1) * BLK)
                z = zs[at, i * rows:(i + 1) * rows]
                peak = jnp.max(z, axis=0, keepdims=True)
                value = jnp.exp2((z - peak) * (scale * log2e))
                e[c, at, :] = value
                mloc[c, j:j + 1, :] = peak * scale
                sums.append(jnp.sum(value, axis=0, keepdims=True))
            w = weights(s, c)
            peaks = jnp.where(w > 0.0, mloc[c], NEG)
            top = jnp.max(peaks, axis=0, keepdims=True)
            total = jnp.concatenate(sums, axis=0) * jnp.exp(peaks - top)
            total = jnp.sum(jnp.where(w > 0.0, w * total, 0.0), axis=0, keepdims=True)
            stat_out[s, 0, pl.ds(a, 1), :] = top
            stat_out[s, 0, pl.ds(RING + a, 1), :] = total

    def stat_copy(s, stage):
        base = s * stat_messages + stage * len(near)
        return [
            remote(base + i, stat_out.at[s, stage], stat_in.at[s, stage, i], device)
            for i, device in enumerate(across if stage else near)
        ]

    def stat_send(s, stage):
        for copy in stat_copy(s, stage):
            copy.start()

    def stat_merge(s, stage):
        copies = stat_copy(s, stage)
        for copy in copies:
            copy.wait_recv()
        got = [stat_out[s, stage]] + [stat_in[s, stage, i] for i in range(len(copies))]
        tops = [v[:RING] for v in got]
        top = functools.reduce(jnp.maximum, tops)
        total = sum(v[RING:] * jnp.exp(p - top) for v, p in zip(got, tops))
        if stage == 0:
            stat_out[s, 1, :RING, :] = top
            stat_out[s, 1, RING:, :] = total
            stat_send(s, 1)
            return
        lse[s, :RING, :] = top + jnp.log(total)
        for a in range(RING):
            c = s * RING + a
            scaled = jnp.exp(mloc[c] - lse[s, a:a + 1, :])
            w = weights(s, c)
            factor[c] = jnp.where(keep[c] > 0.0, scaled, 0.0)
            factor_w[c] = jnp.where(w > 0.0, w * scaled, 0.0)

    def ring1(s, i):
        right, left = first(1), first(3)
        low, high = pl.ds(0, half), pl.ds(half, half)
        src, device = [
            (t.at[s, 0, low], right), (t.at[s, 0, high], left),
            (t.at[s, 1, high], right), (t.at[s, 1, low], right),
            (t.at[s, 2, low], left), (t.at[s, 2, high], left),
        ][i]
        return remote(base0 + s * 13 + i, src, r1.at[s, i], device)

    def terms(s, k):
        hop = jnp.where(k == 0, 2, jnp.where(k == 1, 1, jnp.where(k == 2, 3, 0)))
        a = (own_a + hop) % RING
        c = s * RING + a
        place = posx[c, 0:1, :]
        for j in range(blocks):
            at = slice(j * BLK, (j + 1) * BLK)
            value = e[c, at, :] * factor_w[c, j:j + 1, :]
            if j < slab_blocks:
                row = lax.broadcasted_iota(jnp.int32, (BLK, rows), 0) + j * BLK
                value = value - jnp.where(row == place, 1.0, 0.0)
            ah[at, :], al[at, :] = halves(value)
        t[s, k] = mm(ah[...], chi[s], TN) + mm(ah[...], clo[s], TN) + mm(al[...], chi[s], TN)

    def push(s, *which):
        for i in which:
            ring1(s, i).start()

    def relay1(s):
        ring1(s, 0).wait_recv()
        t[s, 1, :half, :] += r1[s, 0]
        ring1(s, 3).start()
        ring1(s, 1).wait_recv()
        t[s, 2, half:, :] += r1[s, 1]
        ring1(s, 5).start()

    def piece(s, d, side):
        at = ((own_b + d) % RING) * quarter + side * part
        return u.at[s, pl.ds(pl.multiple_of(at, part), part)]

    def ring2(s, i):
        right, left = second(1), second(3)
        d, side, device = [(2, 0, right), (2, 1, left), (1, 1, right), (1, 0, right), (3, 0, left), (3, 1, left)][i]
        return remote(base0 + s * 13 + 6 + i, piece(s, d, side), r2.at[s, i], device)

    def finish1(s):
        for i in (2, 3, 4, 5):
            ring1(s, i).wait_recv()
        u[s, :half, :] = t[s, 3, :half, :] + r1[s, 3] + r1[s, 4]
        u[s, half:, :] = t[s, 3, half:, :] + r1[s, 2] + r1[s, 5]
        for i in (0, 1, 2, 4):
            ring2(s, i).start()

    def relay2(s):
        ring2(s, 0).wait_recv()
        ref = piece(s, 1, 0)
        ref[...] += r2[s, 0]
        ring2(s, 3).start()
        ring2(s, 1).wait_recv()
        ref = piece(s, 3, 1)
        ref[...] += r2[s, 1]
        ring2(s, 5).start()

    def last(s):
        return remote(base0 + s * 13 + 12, piece(s, 0, 1 - zl), r3.at[s], z_peer)

    def finish2(s):
        for i in (2, 3, 4, 5):
            ring2(s, i).wait_recv()
        ref = piece(s, 0, 0)
        ref[...] += r2[s, 3] + r2[s, 4]
        ref = piece(s, 0, 1)
        ref[...] += r2[s, 2] + r2[s, 5]
        last(s).start()

    def finish3(s):
        last(s).wait_recv()
        ref = piece(s, 0, zl)
        ref[...] += r3[s]
        out_copy(s).start()

    def out_copy(s):
        return pltpu.make_async_copy(piece(s, 0, zl), qg_hbm.at[s], out_sem.at[s])

    side = cols // 2
    pieces = side // BLK
    base = base0 + steps * 13

    def spot(which, p):
        return pl.ds(pl.multiple_of(which * side + p * BLK, BLK), BLK)

    def pair_copy(p):
        return remote(base + p, g.at[spot(1 - core, p)], pair_in.at[p], pair_peer)

    def far_copy(p):
        return remote(base + pieces + p, g.at[spot(core, p)], far_in.at[p], far_peer)

    def final_copy(p):
        at = spot(core, p)
        return remote(base + 2 * pieces + p, g.at[at], cg_hbm.at[at], pair_peer)

    def final_local(p):
        at = spot(core, p)
        return pltpu.make_async_copy(g.at[at], cg_hbm.at[at], out_sem.at[steps + p])

    def gradient(p, _):
        for i, which in enumerate((1 - core, core)):
            for c in range(steps * RING):
                scaled = factor[c, pl.ds(which * pieces + p, 1), :]
                put = (slice(i * BLK, (i + 1) * BLK), slice(c * rows, (c + 1) * rows))
                dh[put], dl[put] = halves(e[c, spot(which, p), :] * scaled)
        every = q[...].reshape(steps * RING * rows, width)
        both = mm(dh[...], every, NN) + mm(dl[...], every, NN)
        g[spot(1 - core, p), :] = both[:BLK]
        g[spot(core, p), :] = both[BLK:]
        pair_copy(p).start()

    def pair_add(p):
        pair_copy(p).wait_recv()
        g[spot(core, p), :] += pair_in[p]
        far_copy(p).start()

    def far_add(p):
        far_copy(p).wait()
        g[spot(core, p), :] += far_in[p]
        final_copy(p).start()
        final_local(p).start()

    def q_ready(s):
        pltpu.make_async_copy(q_hbm.at[s], q.at[s], in_sem.at[q_sem + s]).wait()

    tables(0)
    load_c.wait()
    for load in loads_f:
        load.wait()
    for s in range(1, steps):
        load_q(s)
    prepare(0, 1)
    q_ready(0)
    pl.semaphore_wait(barrier, len(peers))

    plan = [
        ("s", 0, 0, []),
        ("s", 0, 1, [(stat_send, 0, 0), (prepare, 1, steps), (tables, 1), (tables, 2), (q_ready, 1), (q_ready, 2)]),
        ("s", 1, 0, [(stat_merge, 0, 0)]),
        ("s", 1, 1, [(stat_send, 1, 0), (stat_merge, 0, 1)]),
        ("t", 0, 0, [(push, 0, 0, 1)]),
        ("s", 2, 0, [(stat_merge, 1, 0)]),
        ("s", 2, 1, [(stat_send, 2, 0)]),
        ("t", 0, 1, [(stat_merge, 2, 0), (push, 0, 2), (stat_merge, 1, 1)]),
        ("t", 0, 2, [(push, 0, 4)]),
        ("t", 0, 3, [(relay1, 0), (stat_merge, 2, 1)]),
        ("g", 0, 0, []),
        ("t", 1, 0, [(push, 1, 0, 1), (pair_add, 0)]),
        ("t", 1, 1, [(push, 1, 2)]),
        ("t", 1, 2, [(push, 1, 4)]),
        ("g", 1, 0, [(finish1, 0)]),
        ("t", 1, 3, [(relay1, 1), (pair_add, 1)]),
        ("t", 2, 0, [(push, 2, 0, 1), (relay2, 0)]),
        ("t", 2, 1, [(push, 2, 2)]),
        ("g", 2, 0, []),
        ("t", 2, 2, [(push, 2, 4), (finish2, 0), (pair_add, 2)]),
        ("t", 2, 3, []),
        ("g", 3, 0, [(finish1, 1)]),
    ]

    @pl.loop(0, len(plan))
    def _(n):
        for name, work in (("s", scores), ("t", terms), ("g", gradient)):
            mine = [(i, entry) for i, entry in enumerate(plan) if entry[0] == name]

            @pl.when(functools.reduce(jnp.logical_or, [n == i for i, _ in mine]))
            def _(mine=mine, work=work):
                work(sum(jnp.where(n == i, entry[1], 0) for i, entry in mine), sum(jnp.where(n == i, entry[2], 0) for i, entry in mine))

        for i, entry in enumerate(plan):
            if entry[3]:
                @pl.when(n == i)
                def _(todo=entry[3]):
                    for call, *args in todo:
                        call(*args)

    pair_add(3)
    far_add(0)
    relay2(1)
    relay1(2)
    far_add(1)
    finish2(1)
    finish3(0)
    far_add(2)
    finish1(2)
    relay2(2)
    finish3(1)
    finish2(2)
    far_add(3)
    finish3(2)
    for s in range(steps):
        for stage in range(2):
            for copy in stat_copy(s, stage):
                copy.wait_send()
        for i in range(6):
            ring1(s, i).wait_send()
            ring2(s, i).wait_send()
        last(s).wait_send()
        out_copy(s).wait()
    for p in range(pieces):
        pair_copy(p).wait_send()
        final_local(p).wait()
        final_copy(p).wait()


def publish(a_ref, b_ref, a_out, b_out, a_buf, b_buf, sems):
    tiles = b_ref.shape[0] // BLK

    def moves(src, buf, dst):
        def at(i):
            return pl.ds(i * BLK, BLK)

        first = [pltpu.make_async_copy(src.at[at(i)], buf.at[at(i)], sems.at[0, i]) for i in range(tiles)]
        second = [pltpu.make_async_copy(buf.at[at(i)], dst.at[at(i)], sems.at[1, i]) for i in range(tiles)]
        return first, second

    first, second = moves(b_ref, b_buf, b_out)
    first.append(pltpu.make_async_copy(a_ref, a_buf, sems.at[0, tiles]))
    second.append(pltpu.make_async_copy(a_buf, a_out, sems.at[1, tiles]))
    for copy in first:
        copy.start()
    for one, two in zip(first, second):
        one.wait()
        two.start()
    for copy in second:
        copy.wait()


def on_device(queries, positives, block_list, block_count, refresh_owner, cache, fresh):
    steps, group_rows, width = queries.shape
    cols = cache.shape[0]
    owners = lax.axis_size("cache")
    share = group_rows // owners
    rows = group_rows // RING
    chunks = steps * RING
    blocks = cols // BLK
    half, part = rows // 2, rows // RING // 2
    pieces = cols // 2 // BLK
    messages = steps * 23 + 3 * pieces
    vmem = pl.BlockSpec(memory_space=pltpu.VMEM)
    smem = pl.BlockSpec(memory_space=pltpu.SMEM)
    anywhere = pl.BlockSpec(memory_space=pl.ANY)
    small = pltpu.VMEM((chunks, blocks, rows), F32)
    a, b = pl.pallas_call(
        kernel,
        out_shape=(
            jax.ShapeDtypeStruct((steps, share, width), F32),
            jax.ShapeDtypeStruct((cols, width), F32),
        ),
        in_specs=[anywhere, vmem, vmem, smem, smem, anywhere, anywhere],
        out_specs=(anywhere, anywhere),
        scratch_shapes=[
            pltpu.VMEM((steps, group_rows, width), BF16),
            pltpu.VMEM((steps, cols, width), BF16),
            pltpu.VMEM((steps, cols, width), BF16),
            pltpu.VMEM((chunks, cols, rows), F32),
            pltpu.VMEM((cols, 2 * rows), F32),
            pltpu.VMEM((cols, rows), BF16),
            pltpu.VMEM((cols, rows), BF16),
            pltpu.VMEM((2 * BLK, chunks * rows), BF16),
            pltpu.VMEM((2 * BLK, chunks * rows), BF16),
            small, small, small, small,
            pltpu.VMEM((chunks, 8, rows), jnp.int32),
            pltpu.VMEM((steps, 8, rows), F32),
            pltpu.VMEM((steps, 2, 8, rows), F32),
            pltpu.VMEM((steps, 2, 7, 8, rows), F32),
            pltpu.VMEM((steps, RING, rows, width), F32),
            pltpu.VMEM((steps, 6, half, width), F32),
            pltpu.VMEM((steps, rows, width), F32),
            pltpu.VMEM((steps, 6, part, width), F32),
            pltpu.VMEM((steps, part, width), F32),
            pltpu.VMEM((cols, width), F32),
            pltpu.VMEM((pieces, BLK, width), F32),
            pltpu.VMEM((pieces, BLK, width), F32),
            pltpu.SemaphoreType.DMA((1 + fresh.shape[0] // rows + steps,)),
            pltpu.SemaphoreType.DMA((steps + pieces,)),
            pltpu.SemaphoreType.DMA((messages,)),
            pltpu.SemaphoreType.DMA((messages,)),
        ],
        compiler_params=pltpu.CompilerParams(
            collective_id=0, has_side_effects=True, vmem_limit_bytes=67_043_328
        ),
        name="cache_step",
    )(queries, positives, block_list, block_count, refresh_owner, cache, fresh)
    return pl.pallas_call(
        publish,
        out_shape=(jax.ShapeDtypeStruct(a.shape, F32), jax.ShapeDtypeStruct(b.shape, F32)),
        in_specs=[anywhere, anywhere],
        out_specs=(anywhere, anywhere),
        scratch_shapes=[
            pltpu.VMEM(a.shape, F32),
            pltpu.VMEM(b.shape, F32),
            pltpu.SemaphoreType.DMA((2, cols // BLK + 1)),
        ],
        name="publish",
    )(a, b)


def solution(mesh):
    return jax.shard_map(
        on_device,
        mesh=mesh,
        in_specs=(
            P(None, "batch", None),
            P(None, "batch"),
            P(None, "batch", None),
            P(None, "batch"),
            P(),
            P("cache", None),
            P("cache", None),
        ),
        out_specs=(P(None, ("batch", "cache"), None), P("cache", None)),
        check_vma=False,
    )
```

```python
import functools
import math

import jax
import jax.numpy as jnp
from jax import lax
from jax.experimental import pallas as pl
from jax.experimental.pallas import tpu as pltpu
from jax.sharding import PartitionSpec as P

BLK = 128
RING = 4
NEG = -1e30
F32 = jnp.float32
BF16 = jnp.bfloat16
NT = (((1,), (1,)), ((), ()))
TN = (((0,), (0,)), ((), ()))
NN = (((1,), (0,)), ((), ()))
ORDER = (2, 1, 3, 0)


def mm(a, b, dims):
    return lax.dot_general(a, b, dims, preferred_element_type=F32)


def halves(x):
    high = x.astype(BF16)
    return high, (x - high.astype(F32)).astype(BF16)


def kernel(
    split, q_hbm, pos_ref, list_ref, count_ref, owner_ref, cache_hbm, fresh_hbm,
    qg_hbm, cg_hbm,
    q, chi, clo, e, zs, ah, al, dh, dl, mloc, keep, factor, factor_w, posx, lse,
    stat_out, stat_in, t, r1, u, r2, r3, g, pair_in, far_in,
    in_sem, out_sem, send_sem, recv_sem,
):
    steps = q.shape[0]
    rows = q.shape[1] // RING
    width = q.shape[2]
    cols = chi.shape[1]
    blocks = cols // BLK
    slab = fresh_hbm.shape[0]
    slab_blocks = slab // BLK
    quarter = rows // RING
    part = quarter // 2
    half = rows // 2
    list_width = list_ref.shape[2]
    scale = 2.0 / math.sqrt(width)
    flows = [(s, pl.ds(0, width)) for s in range(steps - 1)]
    flows += [(steps - 1, pl.ds(0, split)), (steps - 1, pl.ds(split, width - split))]
    log2e = math.log2(math.e)

    ci = lax.axis_index("cache")
    bi = lax.axis_index("batch")
    x, y, zl = ci // 8, (ci // 2) % 4, ci % 2
    zh, core = bi // 2, bi % 2
    one, two = 1 - core, core
    own_a = x * one + y * two
    own_b = y * one + x * two

    def first(d):
        return (((x + d * one) % 4) * 8 + ((y + d * two) % 4) * 2 + zl, bi)

    def second(d):
        return (((x + d * two) % 4) * 8 + ((y + d * one) % 4) * 2 + zl, bi)

    def flip(device):
        return (device[0] + 1 - 2 * zl, device[1])

    z_peer = flip((ci, bi))
    far_peer = (ci, (1 - zh) * 2 + core)
    pair_peer = (ci, zh * 2 + 1 - core)
    near = [second(1), second(2), second(3), z_peer, flip(second(1)), flip(second(2)), flip(second(3))]
    across = [first(1), first(2), first(3)]
    peers = near + across + [far_peer, pair_peer]

    def remote(number, src, dst, device):
        return pltpu.make_async_remote_copy(
            src_ref=src, dst_ref=dst, send_sem=send_sem.at[number], recv_sem=recv_sem.at[number],
            device_id=device, device_id_type=pl.DeviceIdType.MESH,
        )

    stat_messages = len(near) + len(across)
    base0 = steps * stat_messages
    barrier = pltpu.get_barrier_semaphore()
    for peer in peers:
        pl.semaphore_signal(barrier, inc=1, device_id=peer, device_id_type=pl.DeviceIdType.MESH)

    load_c = pltpu.make_async_copy(cache_hbm, g, in_sem.at[0])
    load_c.start()
    loads_f = []
    for i in range(slab // rows):
        loads_f.append(pltpu.make_async_copy(fresh_hbm.at[pl.ds(i * rows, rows)], u.at[i], in_sem.at[1 + i]))
        loads_f[-1].start()
    q_sem = 1 + slab // rows

    def load_q(s):
        @pl.loop(0, RING * RING)
        def _(i):
            a, b = i // RING, i % RING
            src = (a * one + b * two) * rows + (b * one + a * two) * quarter
            pltpu.make_async_copy(
                q_hbm.at[s, pl.ds(pl.multiple_of(src, quarter), quarter)],
                q.at[s, pl.ds(pl.multiple_of(i * quarter, quarter), quarter)],
                in_sem.at[q_sem + s],
            ).start()

    for s in range(steps):
        load_q(s)

    lanes = lax.broadcasted_iota(jnp.int32, (blocks, rows), 1)
    slot = lax.broadcasted_iota(jnp.int32, (1, list_width), 1)
    ids = ci * blocks + lax.broadcasted_iota(jnp.int32, (blocks, 1), 0)
    low_lanes = lax.broadcasted_iota(jnp.int32, (8, BLK), 1) < quarter

    def tables(s):
        @pl.loop(0, RING)
        def _(a):
            c = s * RING + a
            listed = jnp.zeros((blocks, rows), F32)
            picked = []
            for b in range(RING):
                block = (2 * a + b // 2) * one + (2 * b + a // 2) * two
                row = list_ref[s, pl.ds(block, 1), :]
                valid = slot < count_ref[s, block]
                hit = jnp.where((row == ids) & valid, 1.0, 0.0)
                hit = jnp.max(hit, axis=1, keepdims=True)
                listed = jnp.where(lanes // quarter == b, hit, listed)
                tile = (2 * a + b // 2) * one + (2 * b + a // 2) * two
                found = pos_ref[pl.ds(s, 1), pl.ds(pl.multiple_of(tile * BLK, BLK), BLK)]
                found = jnp.broadcast_to(found, (8, BLK))
                side = (b % 2) * one + (a % 2) * two
                flag = jnp.broadcast_to(side, (8, BLK)) == b % 2
                picked.append(jnp.where(flag, found, pltpu.roll(found, quarter, 1)))
            keep[c] = listed
            mine = jnp.broadcast_to(owner_ref[s], (8, BLK)) == ci
            for i in range(2):
                both = jnp.where(low_lanes, picked[2 * i], picked[2 * i + 1])
                posx[c, :, i * BLK:(i + 1) * BLK] = jnp.where(mine, both, -1)

    def weights(s, c):
        mine = jnp.broadcast_to(owner_ref[s], (blocks, rows)) == ci
        top = lax.broadcasted_iota(jnp.int32, (blocks, rows), 0) < slab_blocks
        return keep[c] + jnp.where(mine & top, 1.0, 0.0)

    def prepare(begin, end):
        @pl.loop(slab // BLK, cols // BLK)
        def _(i):
            at = pl.ds(pl.multiple_of(i * BLK, BLK), BLK)
            high, low = halves(g[at, :])
            for s in range(begin, end):
                chi[s, at, :] = high
                clo[s, at, :] = low

        @pl.loop(0, slab // BLK)
        def _(i):
            at = pl.ds(pl.multiple_of(i * BLK, BLK), BLK)
            per = rows // BLK
            old = g[at, :]
            new = u[i // per, pl.ds(pl.multiple_of((i % per) * BLK, BLK), BLK), :]
            done = jnp.zeros((BLK, width), jnp.bool_)
            for s in range(end):
                done = done | (jnp.broadcast_to(owner_ref[s], (BLK, width)) == ci)
                if s >= begin:
                    high, low = halves(jnp.where(done, new, old))
                    chi[s, at, :] = high
                    clo[s, at, :] = low

    def scores(count):
        s, h = count // 2, count % 2
        block_q = q[s, pl.ds(pl.multiple_of(h * 2 * rows, 2 * rows), 2 * rows), :]
        zs[...] = mm(chi[s], block_q, NT) + mm(clo[s], block_q, NT)
        for i in range(2):
            a = 2 * h + i
            c = s * RING + a
            sums = []
            for j in range(blocks):
                at = slice(j * BLK, (j + 1) * BLK)
                z = zs[at, i * rows:(i + 1) * rows]
                peak = jnp.max(z, axis=0, keepdims=True)
                value = jnp.exp2((z - peak) * (scale * log2e))
                e[c, at, :] = value
                mloc[c, j:j + 1, :] = peak * scale
                sums.append(jnp.sum(value, axis=0, keepdims=True))
            w = weights(s, c)
            peaks = jnp.where(w > 0.0, mloc[c], NEG)
            top = jnp.max(peaks, axis=0, keepdims=True)
            total = jnp.concatenate(sums, axis=0) * jnp.exp(peaks - top)
            total = jnp.sum(jnp.where(w > 0.0, w * total, 0.0), axis=0, keepdims=True)
            stat_out[s, 0, pl.ds(a, 1), :] = top
            stat_out[s, 0, pl.ds(RING + a, 1), :] = total

    def stat_copy(s, stage):
        base = s * stat_messages + stage * len(near)
        return [
            remote(base + i, stat_out.at[s, stage], stat_in.at[s, stage, i], device)
            for i, device in enumerate(across if stage else near)
        ]

    def stat_send(s, stage):
        for copy in stat_copy(s, stage):
            copy.start()

    def stat_merge(s, stage):
        copies = stat_copy(s, stage)
        for copy in copies:
            copy.wait_recv()
        got = [stat_out[s, stage]] + [stat_in[s, stage, i] for i in range(len(copies))]
        tops = [v[:RING] for v in got]
        top = functools.reduce(jnp.maximum, tops)
        total = sum(v[RING:] * jnp.exp(p - top) for v, p in zip(got, tops))
        if stage == 0:
            stat_out[s, 1, :RING, :] = top
            stat_out[s, 1, RING:, :] = total
            stat_send(s, 1)
            return
        lse[s, :RING, :] = top + jnp.log(total)
        for a in range(RING):
            c = s * RING + a
            scaled = jnp.exp(mloc[c] - lse[s, a:a + 1, :])
            w = weights(s, c)
            factor[c] = jnp.where(keep[c] > 0.0, scaled, 0.0)
            factor_w[c] = jnp.where(w > 0.0, w * scaled, 0.0)

    def ring1(f, i):
        s, along = flows[f]
        number = base0 + f * 13 + i
        if f == 0 and i in (3, 5, 6, 7):
            along = pl.ds(0 if i < 6 else width // 2, width // 2)
            if i >= 6:
                number, i = base0 + len(flows) * 13 + 3 * (cols // 2 // BLK) + i - 6, 2 * i - 9
        right, left = first(1), first(3)
        low, high = pl.ds(0, half), pl.ds(half, half)
        k, side, device = [(0, low, right), (0, high, left), (1, high, right), (1, low, right), (2, low, left), (2, high, left)][i]
        return remote(number, t.at[s, k, side, along], r1.at[s, i, :, along], device)

    def terms(count):
        s, k = count // RING, count % RING
        hop = jnp.where(k == 0, 2, jnp.where(k == 1, 1, jnp.where(k == 2, 3, 0)))
        a = (own_a + hop) % RING
        c = s * RING + a
        place = posx[c, 0:1, :]
        for j in range(blocks):
            at = slice(j * BLK, (j + 1) * BLK)
            value = e[c, at, :] * factor_w[c, j:j + 1, :]
            if j < slab_blocks:
                row = lax.broadcasted_iota(jnp.int32, (BLK, rows), 0) + j * BLK
                value = value - jnp.where(row == place, 1.0, 0.0)
            ah[at, :], al[at, :] = halves(value)
        t[s, k] = mm(ah[...], chi[s], TN) + mm(ah[...], clo[s], TN) + mm(al[...], chi[s], TN)

    def push(f, *which):
        for i in which:
            ring1(f, i).start()

    def add(target, *sources):
        target[...] += functools.reduce(jnp.add, [source[...] for source in sources])

    def relay1(f):
        s, along = flows[f]
        for i, k, side, out in ((0, 1, pl.ds(0, half), 3), (1, 2, pl.ds(half, half), 5)):
            ring1(f, i).wait_recv()
            add(t.at[s, k, side, along], r1.at[s, i, :, along])
            ring1(f, out).start()

    def piece(f, d, side):
        s, along = flows[f]
        at = ((own_b + d) % RING) * quarter + side * part
        return u.at[s, pl.ds(pl.multiple_of(at, part), part), along]

    def ring2(f, i):
        s, along = flows[f]
        right, left = second(1), second(3)
        d, side, device = [(2, 0, right), (2, 1, left), (1, 1, right), (1, 0, right), (3, 0, left), (3, 1, left)][i]
        return remote(base0 + f * 13 + 6 + i, piece(f, d, side), r2.at[s, i, :, along], device)

    def finish1(f):
        s, along = flows[f]
        for i in (2, 3, 4, 5) if f else (2, 3, 4, 5, 6, 7):
            ring1(f, i).wait_recv()
        u[s, :half, along] = t[s, 3, :half, along] + r1[s, 3, :, along] + r1[s, 4, :, along]
        u[s, half:, along] = t[s, 3, half:, along] + r1[s, 2, :, along] + r1[s, 5, :, along]
        for i in (0, 1, 2, 4):
            ring2(f, i).start()

    def relay2(f):
        s, along = flows[f]
        for i, d, side, out in ((0, 1, 0, 3), (1, 3, 1, 5)):
            ring2(f, i).wait_recv()
            add(piece(f, d, side), r2.at[s, i, :, along])
            ring2(f, out).start()

    def last(f):
        s, along = flows[f]
        return remote(base0 + f * 13 + 12, piece(f, 0, 1 - zl), r3.at[s, :, along], z_peer)

    def finish2(f):
        s, along = flows[f]
        for i in (2, 3, 4, 5):
            ring2(f, i).wait_recv()
        add(piece(f, 0, 0), r2.at[s, 3, :, along], r2.at[s, 4, :, along])
        add(piece(f, 0, 1), r2.at[s, 2, :, along], r2.at[s, 5, :, along])
        last(f).start()

    def finish3(f):
        s, along = flows[f]
        last(f).wait_recv()
        add(piece(f, 0, zl), r3.at[s, :, along])
        out_copy(f).start()

    def out_copy(f):
        s, along = flows[f]
        return pltpu.make_async_copy(piece(f, 0, zl), qg_hbm.at[s, :, along], out_sem.at[f])

    side = cols // 2
    pieces = side // BLK
    base = base0 + len(flows) * 13

    def spot(which, p):
        return pl.ds(pl.multiple_of(which * side + p * BLK, BLK), BLK)

    def pair_copy(p):
        return remote(base + p, g.at[spot(1 - core, p)], pair_in.at[p], pair_peer)

    def far_copy(p):
        return remote(base + pieces + p, g.at[spot(core, p)], far_in.at[p], far_peer)

    def final_copy(p):
        at = spot(core, p)
        return remote(base + 2 * pieces + p, g.at[at], cg_hbm.at[at], pair_peer)

    def final_local(p):
        at = spot(core, p)
        return pltpu.make_async_copy(g.at[at], cg_hbm.at[at], out_sem.at[len(flows) + p])

    def gradient(p):
        for i, which in enumerate((1 - core, core)):
            for c in range(steps * RING):
                scaled = factor[c, pl.ds(which * pieces + p, 1), :]
                put = (slice(i * BLK, (i + 1) * BLK), slice(c * rows, (c + 1) * rows))
                dh[put], dl[put] = halves(e[c, spot(which, p), :] * scaled)
        every = q[...].reshape(steps * RING * rows, width)
        both = mm(dh[...], every, NN) + mm(dl[...], every, NN)
        g[spot(1 - core, p), :] = both[:BLK]
        g[spot(core, p), :] = both[BLK:]
        pair_copy(p).start()

    def pair_add(p):
        pair_copy(p).wait_recv()
        g[spot(core, p), :] += pair_in[p]
        far_copy(p).start()

    def far_add(p):
        far_copy(p).wait()
        g[spot(core, p), :] += far_in[p]
        final_copy(p).start()
        final_local(p).start()

    def q_ready(s):
        pltpu.make_async_copy(q_hbm.at[s], q.at[s], in_sem.at[q_sem + s]).wait()

    for s in range(steps):
        tables(s)
    load_c.wait()
    for load in loads_f:
        load.wait()
    prepare(0, 1)
    q_ready(0)
    pl.semaphore_wait(barrier, len(peers))

    plan = [
        ("s", []),
        ("s", [(stat_send, 0, 0), (prepare, 1, steps), (q_ready, 1), (q_ready, 2)]),
        ("s", [(stat_merge, 0, 0)]),
        ("s", [(stat_send, 1, 0), (stat_merge, 0, 1)]),
        ("t", [(push, 0, 0, 1)]),
        ("s", [(stat_merge, 1, 0)]),
        ("t", [(push, 0, 2)]),
        ("t", [(push, 0, 4)]),
        ("s", [(stat_send, 2, 0), (stat_merge, 1, 1), (relay1, 0)]),
        ("t", []),
        ("t", [(stat_merge, 2, 0), (push, 0, 6, 7), (push, 1, 0, 1)]),
        ("t", [(push, 1, 2)]),
        ("t", [(push, 1, 4), (stat_merge, 2, 1)]),
        ("g", [(pair_add, 0)]),
        ("t", [(finish1, 0)]),
        ("t", [(relay1, 1), (push, 2, 0, 1)]),
        ("g", [(pair_add, 1), (relay2, 0)]),
        ("t", [(push, 2, 2)]),
        ("t", [(push, 2, 4), (push, 3, 0, 1)]),
        ("g", [(pair_add, 2), (finish2, 0)]),
        ("t", [(finish1, 1)]),
        ("g", [(relay1, 2), (push, 3, 2, 4), (pair_add, 3)]),
    ]
    group = 6

    def unit(n, counts):
        after = []
        for (name, work), count in zip((("s", scores), ("t", terms), ("g", gradient)), counts):
            bits = sum(1 << i for i, entry in enumerate(plan) if entry[0] == name)
            mine = lax.rem(lax.shift_right_logical(jnp.int32(bits), n), 2)

            @pl.when(mine == 1)
            def _(work=work, count=count):
                work(count)

            after.append(count + mine)
        for begin in range(0, len(plan), group):
            @pl.when((n >= begin) & (n < begin + group))
            def _(begin=begin):
                for i, entry in enumerate(plan[begin:begin + group], begin):
                    if entry[1]:
                        @pl.when(n == i)
                        def _(todo=entry[1]):
                            for call, *args in todo:
                                call(*args)
        return tuple(after)

    lax.fori_loop(0, len(plan), unit, (jnp.int32(0),) * 3)

    far_add(0)
    relay2(1)
    relay1(3)
    far_add(1)
    finish2(1)
    finish1(2)
    finish1(3)
    relay2(2)
    relay2(3)
    finish2(2)
    finish3(0)
    far_add(2)
    finish2(3)
    far_add(3)
    finish3(1)
    for s in range(steps):
        for stage in range(2):
            for copy in stat_copy(s, stage):
                copy.wait_send()
    for f in range(len(flows)):
        for i in range(6 if f else 8):
            ring1(f, i).wait_send()
    for p in range(pieces):
        pair_copy(p).wait_send()
    finish3(2)
    for f in range(steps - 1):
        for i in range(6):
            ring2(f, i).wait_send()
        last(f).wait_send()
        out_copy(f).wait()
    for p in range(pieces):
        final_local(p).wait()
        final_copy(p).wait()
    finish3(3)
    for f in range(steps - 1, len(flows)):
        for i in range(6):
            ring2(f, i).wait_send()
        last(f).wait_send()
        out_copy(f).wait()


def publish(a_ref, b_ref, a_out, b_out, a_buf, b_buf, sems):
    tiles = b_ref.shape[0] // BLK

    def moves(src, buf, dst):
        def at(i):
            return pl.ds(i * BLK, BLK)

        first = [pltpu.make_async_copy(src.at[at(i)], buf.at[at(i)], sems.at[0, i]) for i in range(tiles)]
        second = [pltpu.make_async_copy(buf.at[at(i)], dst.at[at(i)], sems.at[1, i]) for i in range(tiles)]
        return first, second

    first, second = moves(b_ref, b_buf, b_out)
    first.append(pltpu.make_async_copy(a_ref, a_buf, sems.at[0, tiles]))
    second.append(pltpu.make_async_copy(a_buf, a_out, sems.at[1, tiles]))
    for copy in first:
        copy.start()
    for one, two in zip(first, second):
        one.wait()
        two.start()
    for copy in second:
        copy.wait()


def on_device(queries, positives, block_list, block_count, refresh_owner, cache, fresh):
    steps, group_rows, width = queries.shape
    cols = cache.shape[0]
    owners = lax.axis_size("cache")
    share = group_rows // owners
    rows = group_rows // RING
    chunks = steps * RING
    blocks = cols // BLK
    half, part = rows // 2, rows // RING // 2
    pieces = cols // 2 // BLK
    split = width // 3 * 2
    flows = steps + 1
    messages = steps * 10 + flows * 13 + 3 * pieces + 2
    vmem = pl.BlockSpec(memory_space=pltpu.VMEM)
    smem = pl.BlockSpec(memory_space=pltpu.SMEM)
    anywhere = pl.BlockSpec(memory_space=pl.ANY)
    small = pltpu.VMEM((chunks, blocks, rows), F32)
    a, b = pl.pallas_call(
        functools.partial(kernel, split),
        out_shape=(
            jax.ShapeDtypeStruct((steps, share, width), F32),
            jax.ShapeDtypeStruct((cols, width), F32),
        ),
        in_specs=[anywhere, vmem, vmem, smem, smem, anywhere, anywhere],
        out_specs=(anywhere, anywhere),
        scratch_shapes=[
            pltpu.VMEM((steps, group_rows, width), BF16),
            pltpu.VMEM((steps, cols, width), BF16),
            pltpu.VMEM((steps, cols, width), BF16),
            pltpu.VMEM((chunks, cols, rows), F32),
            pltpu.VMEM((cols, 2 * rows), F32),
            pltpu.VMEM((cols, rows), BF16),
            pltpu.VMEM((cols, rows), BF16),
            pltpu.VMEM((2 * BLK, chunks * rows), BF16),
            pltpu.VMEM((2 * BLK, chunks * rows), BF16),
            small, small, small, small,
            pltpu.VMEM((chunks, 8, rows), jnp.int32),
            pltpu.VMEM((steps, 8, rows), F32),
            pltpu.VMEM((steps, 2, 8, rows), F32),
            pltpu.VMEM((steps, 2, 7, 8, rows), F32),
            pltpu.VMEM((steps, RING, rows, width), F32),
            pltpu.VMEM((steps, 6, half, width), F32),
            pltpu.VMEM((steps, rows, width), F32),
            pltpu.VMEM((steps, 6, part, width), F32),
            pltpu.VMEM((steps, part, width), F32),
            pltpu.VMEM((cols, width), F32),
            pltpu.VMEM((pieces, BLK, width), F32),
            pltpu.VMEM((pieces, BLK, width), F32),
            pltpu.SemaphoreType.DMA((1 + fresh.shape[0] // rows + steps,)),
            pltpu.SemaphoreType.DMA((flows + pieces,)),
            pltpu.SemaphoreType.DMA((messages,)),
            pltpu.SemaphoreType.DMA((messages,)),
        ],
        compiler_params=pltpu.CompilerParams(
            collective_id=0, has_side_effects=True, vmem_limit_bytes=67_043_328
        ),
        name="cache_step",
    )(queries, positives, block_list, block_count, refresh_owner, cache, fresh)
    return pl.pallas_call(
        publish,
        out_shape=(jax.ShapeDtypeStruct(a.shape, F32), jax.ShapeDtypeStruct(b.shape, F32)),
        in_specs=[anywhere, anywhere],
        out_specs=(anywhere, anywhere),
        scratch_shapes=[
            pltpu.VMEM(a.shape, F32),
            pltpu.VMEM(b.shape, F32),
            pltpu.SemaphoreType.DMA((2, cols // BLK + 1)),
        ],
        name="publish",
    )(a, b)


def solution(mesh):
    return jax.shard_map(
        on_device,
        mesh=mesh,
        in_specs=(
            P(None, "batch", None),
            P(None, "batch"),
            P(None, "batch", None),
            P(None, "batch"),
            P(),
            P("cache", None),
            P("cache", None),
        ),
        out_specs=(P(None, ("batch", "cache"), None), P("cache", None)),
        check_vma=False,
    )
```

```python
import functools
import math

import jax
import jax.numpy as jnp
from jax import lax
from jax.experimental import pallas as pl
from jax.experimental.pallas import tpu as pltpu
from jax.sharding import PartitionSpec as P

BLK = 128
RING = 4
NEG = -1e30
F32 = jnp.float32
BF16 = jnp.bfloat16
NT = (((1,), (1,)), ((), ()))
TN = (((0,), (0,)), ((), ()))
NN = (((1,), (0,)), ((), ()))
ORDER = (2, 1, 3, 0)


def mm(a, b, dims):
    return lax.dot_general(a, b, dims, preferred_element_type=F32)


def halves(x):
    high = x.astype(BF16)
    return high, (x - high.astype(F32)).astype(BF16)


def kernel(
    split, q_hbm, pos_ref, list_ref, count_ref, owner_ref, cache_hbm, fresh_hbm,
    qg_hbm, cg_hbm,
    q, chi, clo, e, zs, ah, al, dh, dl, mloc, keep, factor, factor_w, posx, lse,
    stat_out, stat_in, t, r1, u, r2, r3, g, pair_in, far_in,
    in_sem, out_sem, send_sem, recv_sem,
):
    steps = q.shape[0]
    rows = q.shape[1] // RING
    width = q.shape[2]
    cols = chi.shape[1]
    blocks = cols // BLK
    slab = fresh_hbm.shape[0]
    slab_blocks = slab // BLK
    quarter = rows // RING
    part = quarter // 2
    half = rows // 2
    list_width = list_ref.shape[2]
    scale = 2.0 / math.sqrt(width)
    flows = [(s, pl.ds(0, width)) for s in range(steps - 1)]
    flows += [(steps - 1, pl.ds(0, split)), (steps - 1, pl.ds(split, width - split))]
    log2e = math.log2(math.e)

    ci = lax.axis_index("cache")
    bi = lax.axis_index("batch")
    x, y, zl = ci // 8, (ci // 2) % 4, ci % 2
    zh, core = bi // 2, bi % 2
    one, two = 1 - core, core
    own_a = x * one + y * two
    own_b = y * one + x * two

    def first(d):
        return (((x + d * one) % 4) * 8 + ((y + d * two) % 4) * 2 + zl, bi)

    def second(d):
        return (((x + d * two) % 4) * 8 + ((y + d * one) % 4) * 2 + zl, bi)

    def flip(device):
        return (device[0] + 1 - 2 * zl, device[1])

    z_peer = flip((ci, bi))
    far_peer = (ci, (1 - zh) * 2 + core)
    pair_peer = (ci, zh * 2 + 1 - core)
    near = [second(1), second(2), second(3), z_peer, flip(second(1)), flip(second(2)), flip(second(3))]
    across = [first(1), first(2), first(3)]
    peers = near + across + [far_peer, pair_peer]

    def remote(out, into, src, dst, device):
        return pltpu.make_async_remote_copy(
            src_ref=src, dst_ref=dst, send_sem=send_sem.at[out], recv_sem=recv_sem.at[into],
            device_id=device, device_id_type=pl.DeviceIdType.MESH,
        )

    out1 = 2 * steps
    out2, out3 = out1 + len(flows), out1 + 2 * len(flows)
    out_pair = out1 + 3 * len(flows)
    in1 = 2 * steps
    in2, in3 = in1 + 3 * len(flows), in1 + 6 * len(flows)
    in_pair = in1 + 7 * len(flows)

    def whole(out, into, ref):
        return remote(out, into, ref, ref, z_peer)

    barrier = pltpu.get_barrier_semaphore()
    for peer in peers:
        pl.semaphore_signal(barrier, inc=1, device_id=peer, device_id_type=pl.DeviceIdType.MESH)

    load_c = pltpu.make_async_copy(cache_hbm, g, in_sem.at[0])
    load_c.start()
    loads_f = []
    for i in range(slab // rows):
        loads_f.append(pltpu.make_async_copy(fresh_hbm.at[pl.ds(i * rows, rows)], u.at[i], in_sem.at[1 + i]))
        loads_f[-1].start()
    q_sem = 1 + slab // rows

    def load_q(s):
        @pl.loop(0, RING * RING)
        def _(i):
            a, b = i // RING, i % RING
            src = (a * one + b * two) * rows + (b * one + a * two) * quarter
            pltpu.make_async_copy(
                q_hbm.at[s, pl.ds(pl.multiple_of(src, quarter), quarter)],
                q.at[s, pl.ds(pl.multiple_of(i * quarter, quarter), quarter)],
                in_sem.at[q_sem + s],
            ).start()

    for s in range(steps):
        load_q(s)

    lanes = lax.broadcasted_iota(jnp.int32, (blocks, rows), 1)
    slot = lax.broadcasted_iota(jnp.int32, (1, list_width), 1)
    ids = ci * blocks + lax.broadcasted_iota(jnp.int32, (blocks, 1), 0)
    low_lanes = lax.broadcasted_iota(jnp.int32, (8, BLK), 1) < quarter

    def tables(s):
        @pl.loop(0, RING)
        def _(a):
            c = s * RING + a
            listed = jnp.zeros((blocks, rows), F32)
            picked = []
            for b in range(RING):
                block = (2 * a + b // 2) * one + (2 * b + a // 2) * two
                row = list_ref[s, pl.ds(block, 1), :]
                valid = slot < count_ref[s, block]
                hit = jnp.where((row == ids) & valid, 1.0, 0.0)
                hit = jnp.max(hit, axis=1, keepdims=True)
                listed = jnp.where(lanes // quarter == b, hit, listed)
                tile = (2 * a + b // 2) * one + (2 * b + a // 2) * two
                found = pos_ref[pl.ds(s, 1), pl.ds(pl.multiple_of(tile * BLK, BLK), BLK)]
                found = jnp.broadcast_to(found, (8, BLK))
                side = (b % 2) * one + (a % 2) * two
                flag = jnp.broadcast_to(side, (8, BLK)) == b % 2
                picked.append(jnp.where(flag, found, pltpu.roll(found, quarter, 1)))
            keep[c] = listed
            mine = jnp.broadcast_to(owner_ref[s], (8, BLK)) == ci
            for i in range(2):
                both = jnp.where(low_lanes, picked[2 * i], picked[2 * i + 1])
                posx[c, :, i * BLK:(i + 1) * BLK] = jnp.where(mine, both, -1)

    def weights(s, c):
        mine = jnp.broadcast_to(owner_ref[s], (blocks, rows)) == ci
        top = lax.broadcasted_iota(jnp.int32, (blocks, rows), 0) < slab_blocks
        return keep[c] + jnp.where(mine & top, 1.0, 0.0)

    def prepare(begin, end):
        @pl.loop(slab // BLK, cols // BLK)
        def _(i):
            at = pl.ds(pl.multiple_of(i * BLK, BLK), BLK)
            high, low = halves(g[at, :])
            for s in range(begin, end):
                chi[s, at, :] = high
                clo[s, at, :] = low

        @pl.loop(0, slab // BLK)
        def _(i):
            at = pl.ds(pl.multiple_of(i * BLK, BLK), BLK)
            per = rows // BLK
            old = g[at, :]
            new = u[i // per, pl.ds(pl.multiple_of((i % per) * BLK, BLK), BLK), :]
            done = jnp.zeros((BLK, width), jnp.bool_)
            for s in range(end):
                done = done | (jnp.broadcast_to(owner_ref[s], (BLK, width)) == ci)
                if s >= begin:
                    high, low = halves(jnp.where(done, new, old))
                    chi[s, at, :] = high
                    clo[s, at, :] = low

    def scores(count):
        s, h = count // 2, count % 2
        block_q = q[s, pl.ds(pl.multiple_of(h * 2 * rows, 2 * rows), 2 * rows), :]
        zs[...] = mm(chi[s], block_q, NT) + mm(clo[s], block_q, NT)
        for i in range(2):
            a = 2 * h + i
            c = s * RING + a
            sums = []
            for j in range(blocks):
                at = slice(j * BLK, (j + 1) * BLK)
                z = zs[at, i * rows:(i + 1) * rows]
                peak = jnp.max(z, axis=0, keepdims=True)
                value = jnp.exp2((z - peak) * (scale * log2e))
                e[c, at, :] = value
                mloc[c, j:j + 1, :] = peak * scale
                sums.append(jnp.sum(value, axis=0, keepdims=True))
            w = weights(s, c)
            peaks = jnp.where(w > 0.0, mloc[c], NEG)
            top = jnp.max(peaks, axis=0, keepdims=True)
            total = jnp.concatenate(sums, axis=0) * jnp.exp(peaks - top)
            total = jnp.sum(jnp.where(w > 0.0, w * total, 0.0), axis=0, keepdims=True)
            stat_out[s, 0, pl.ds(a, 1), :] = top
            stat_out[s, 0, pl.ds(RING + a, 1), :] = total

    def stat_copy(s, stage):
        number = 2 * s + stage
        return [
            remote(number, number, stat_out.at[s, stage], stat_in.at[s, stage, i], device)
            for i, device in enumerate(across if stage else near)
        ]

    def stat_all(s, stage):
        number = 2 * s + stage
        return whole(number, number, stat_in.at[s, stage, pl.ds(0, len(across) if stage else len(near))])

    def stat_send(s, stage):
        for copy in stat_copy(s, stage):
            copy.start()

    def stat_merge(s, stage):
        stat_all(s, stage).wait_recv()
        got = [stat_out[s, stage]] + [stat_in[s, stage, i] for i in range(len(across) if stage else len(near))]
        tops = [v[:RING] for v in got]
        top = functools.reduce(jnp.maximum, tops)
        total = sum(v[RING:] * jnp.exp(p - top) for v, p in zip(got, tops))
        if stage == 0:
            stat_out[s, 1, :RING, :] = top
            stat_out[s, 1, RING:, :] = total
            stat_send(s, 1)
            return
        lse[s, :RING, :] = top + jnp.log(total)
        for a in range(RING):
            c = s * RING + a
            scaled = jnp.exp(mloc[c] - lse[s, a:a + 1, :])
            w = weights(s, c)
            factor[c] = jnp.where(keep[c] > 0.0, scaled, 0.0)
            factor_w[c] = jnp.where(w > 0.0, w * scaled, 0.0)

    def ring1(f, i):
        s, along = flows[f]
        into = in1 + 3 * f + min(i, 2)
        if f == 0 and i in (3, 5, 6, 7):
            along = pl.ds(0 if i < 6 else width // 2, width // 2)
            if i >= 6:
                i = 2 * i - 9
        right, left = first(1), first(3)
        low, high = pl.ds(0, half), pl.ds(half, half)
        k, side, device = [(0, low, right), (0, high, left), (1, high, right), (1, low, right), (2, low, left), (2, high, left)][i]
        return remote(out1 + f, into, t.at[s, k, side, along], r1.at[s, i, :, along], device)

    def arrived(f, into, ref):
        s, along = flows[f]
        whole(0, into + 3 * f + 2, ref.at[s, pl.ds(2, 4), :, along]).wait_recv()

    def left(f, out, ref):
        s, along = flows[f]
        whole(out + f, 0, ref.at[s, :, :, along]).wait_send()

    def terms(count):
        s, k = count // RING, count % RING
        hop = jnp.where(k == 0, 2, jnp.where(k == 1, 1, jnp.where(k == 2, 3, 0)))
        a = (own_a + hop) % RING
        c = s * RING + a
        place = posx[c, 0:1, :]
        for j in range(blocks):
            at = slice(j * BLK, (j + 1) * BLK)
            value = e[c, at, :] * factor_w[c, j:j + 1, :]
            if j < slab_blocks:
                row = lax.broadcasted_iota(jnp.int32, (BLK, rows), 0) + j * BLK
                value = value - jnp.where(row == place, 1.0, 0.0)
            ah[at, :], al[at, :] = halves(value)
        t[s, k] = mm(ah[...], chi[s], TN) + mm(ah[...], clo[s], TN) + mm(al[...], chi[s], TN)

    def push(f, *which):
        for i in which:
            ring1(f, i).start()

    def add(target, *sources):
        target[...] += functools.reduce(jnp.add, [source[...] for source in sources])

    def relay1(f):
        s, along = flows[f]
        for i, k, side, out in ((0, 1, pl.ds(0, half), 3), (1, 2, pl.ds(half, half), 5)):
            ring1(f, i).wait_recv()
            add(t.at[s, k, side, along], r1.at[s, i, :, along])
            ring1(f, out).start()

    def piece(f, d, side):
        s, along = flows[f]
        at = ((own_b + d) % RING) * quarter + side * part
        return u.at[s, pl.ds(pl.multiple_of(at, part), part), along]

    def ring2(f, i):
        s, along = flows[f]
        right, left = second(1), second(3)
        d, side, device = [(2, 0, right), (2, 1, left), (1, 1, right), (1, 0, right), (3, 0, left), (3, 1, left)][i]
        return remote(out2 + f, in2 + 3 * f + min(i, 2), piece(f, d, side), r2.at[s, i, :, along], device)

    def finish1(f):
        s, along = flows[f]
        arrived(f, in1, r1)
        u[s, :half, along] = t[s, 3, :half, along] + r1[s, 3, :, along] + r1[s, 4, :, along]
        u[s, half:, along] = t[s, 3, half:, along] + r1[s, 2, :, along] + r1[s, 5, :, along]
        for i in (0, 1, 2, 4):
            ring2(f, i).start()

    def relay2(f):
        s, along = flows[f]
        for i, d, side, out in ((0, 1, 0, 3), (1, 3, 1, 5)):
            ring2(f, i).wait_recv()
            add(piece(f, d, side), r2.at[s, i, :, along])
            ring2(f, out).start()

    def last(f):
        s, along = flows[f]
        return remote(out3 + f, in3 + f, piece(f, 0, 1 - zl), r3.at[s, :, along], z_peer)

    def finish2(f):
        s, along = flows[f]
        arrived(f, in2, r2)
        add(piece(f, 0, 0), r2.at[s, 3, :, along], r2.at[s, 4, :, along])
        add(piece(f, 0, 1), r2.at[s, 2, :, along], r2.at[s, 5, :, along])
        last(f).start()

    def finish3(f):
        s, along = flows[f]
        last(f).wait_recv()
        add(piece(f, 0, zl), r3.at[s, :, along])
        out_copy(f).start()

    def out_copy(f):
        s, along = flows[f]
        return pltpu.make_async_copy(piece(f, 0, zl), qg_hbm.at[s, :, along], out_sem.at[f])

    side = cols // 2
    pieces = side // BLK

    def spot(which, p):
        return pl.ds(pl.multiple_of(which * side + p * BLK, BLK), BLK)

    def pair_copy(p):
        return remote(out_pair, in_pair + p, g.at[spot(1 - core, p)], pair_in.at[p], pair_peer)

    def far_copy(p):
        return remote(out_pair + 2 + p, in_pair + pieces + p, g.at[spot(core, p)], far_in.at[p], far_peer)

    def final_copy(p):
        at = spot(core, p)
        return remote(out_pair + 1, in_pair + 2 * pieces, g.at[at], cg_hbm.at[at], pair_peer)

    def final_local(p):
        at = spot(core, p)
        return pltpu.make_async_copy(g.at[at], cg_hbm.at[at], out_sem.at[len(flows)])

    def gradient(p):
        for i, which in enumerate((1 - core, core)):
            for c in range(steps * RING):
                scaled = factor[c, pl.ds(which * pieces + p, 1), :]
                put = (slice(i * BLK, (i + 1) * BLK), slice(c * rows, (c + 1) * rows))
                dh[put], dl[put] = halves(e[c, spot(which, p), :] * scaled)
        every = q[...].reshape(steps * RING * rows, width)
        both = mm(dh[...], every, NN) + mm(dl[...], every, NN)
        g[spot(1 - core, p), :] = both[:BLK]
        g[spot(core, p), :] = both[BLK:]
        pair_copy(p).start()

    def pair_add(p):
        pair_copy(p).wait_recv()
        g[spot(core, p), :] += pair_in[p]
        far_copy(p).start()

    def far_add(p):
        far_copy(p).wait()
        g[spot(core, p), :] += far_in[p]
        final_copy(p).start()
        final_local(p).start()

    def q_ready(s):
        pltpu.make_async_copy(q_hbm.at[s], q.at[s], in_sem.at[q_sem + s]).wait()

    for s in range(steps):
        tables(s)
    load_c.wait()
    for load in loads_f:
        load.wait()
    prepare(0, 1)
    q_ready(0)
    pl.semaphore_wait(barrier, len(peers))

    plan = [
        ("s", []),
        ("s", [(stat_send, 0, 0), (prepare, 1, steps), (q_ready, 1), (q_ready, 2)]),
        ("s", [(stat_merge, 0, 0)]),
        ("s", [(stat_send, 1, 0), (stat_merge, 0, 1)]),
        ("t", [(push, 0, 0, 1)]),
        ("s", [(stat_merge, 1, 0)]),
        ("s", [(stat_send, 2, 0)]),
        ("t", [(push, 0, 2)]),
        ("t", [(push, 0, 4), (stat_merge, 2, 0), (relay1, 0), (push, 0, 6, 7)]),
        ("t", [(stat_merge, 1, 1)]),
        ("t", [(push, 1, 0, 1)]),
        ("t", [(push, 1, 2), (stat_merge, 2, 1)]),
        ("g", [(pair_add, 0)]),
        ("t", [(push, 1, 4)]),
        ("t", [(finish1, 0)]),
        ("t", [(relay1, 1), (push, 2, 0, 1)]),
        ("g", [(pair_add, 1), (relay2, 0)]),
        ("t", [(push, 2, 2)]),
        ("t", [(push, 2, 4), (push, 3, 0, 1)]),
        ("g", [(pair_add, 2), (finish2, 0)]),
        ("t", [(finish1, 1)]),
        ("g", [(relay1, 2), (push, 3, 2, 4), (pair_add, 3)]),
    ]
    group = 6

    def unit(n, counts):
        after = []
        for (name, work), count in zip((("s", scores), ("t", terms), ("g", gradient)), counts):
            bits = sum(1 << i for i, entry in enumerate(plan) if entry[0] == name)
            mine = lax.rem(lax.shift_right_logical(jnp.int32(bits), n), 2)

            @pl.when(mine == 1)
            def _(work=work, count=count):
                work(count)

            after.append(count + mine)
        for begin in range(0, len(plan), group):
            @pl.when((n >= begin) & (n < begin + group))
            def _(begin=begin):
                for i, entry in enumerate(plan[begin:begin + group], begin):
                    if entry[1]:
                        @pl.when(n == i)
                        def _(todo=entry[1]):
                            for call, *args in todo:
                                call(*args)
        return tuple(after)

    lax.fori_loop(0, len(plan), unit, (jnp.int32(0),) * 3)

    far_add(0)
    relay2(1)
    relay1(3)
    far_add(1)
    finish2(1)
    finish1(2)
    finish1(3)
    relay2(2)
    relay2(3)
    finish2(2)
    finish3(0)
    far_add(2)
    finish2(3)
    far_add(3)
    finish3(1)
    for s in range(steps):
        for stage in range(2):
            stat_all(s, stage).wait_send()
    for f in range(len(flows)):
        left(f, out1, r1)
    whole(out_pair, 0, pair_in).wait_send()
    finish3(2)
    for f in range(steps - 1):
        left(f, out2, r2)
        last(f).wait_send()
        out_copy(f).wait()
    mine = pl.ds(pl.multiple_of(core * side, side), side)
    rest = pl.ds(pl.multiple_of((1 - core) * side, side), side)
    pltpu.make_async_copy(g.at[mine], cg_hbm.at[mine], out_sem.at[len(flows)]).wait()
    remote(out_pair + 1, in_pair + 2 * pieces, g.at[mine], cg_hbm.at[rest], pair_peer).wait()
    finish3(3)
    for f in range(steps - 1, len(flows)):
        left(f, out2, r2)
        last(f).wait_send()
        out_copy(f).wait()


def publish(a_ref, b_ref, a_out, b_out, a_buf, b_buf, sems):
    tiles = b_ref.shape[0] // BLK

    def moves(src, buf, dst):
        def at(i):
            return pl.ds(i * BLK, BLK)

        first = [pltpu.make_async_copy(src.at[at(i)], buf.at[at(i)], sems.at[0, i]) for i in range(tiles)]
        second = [pltpu.make_async_copy(buf.at[at(i)], dst.at[at(i)], sems.at[1, i]) for i in range(tiles)]
        return first, second

    first, second = moves(b_ref, b_buf, b_out)
    first.append(pltpu.make_async_copy(a_ref, a_buf, sems.at[0, tiles]))
    second.append(pltpu.make_async_copy(a_buf, a_out, sems.at[1, tiles]))
    for copy in first:
        copy.start()
    for one, two in zip(first, second):
        one.wait()
        two.start()
    for copy in second:
        copy.wait()


def on_device(queries, positives, block_list, block_count, refresh_owner, cache, fresh):
    steps, group_rows, width = queries.shape
    cols = cache.shape[0]
    owners = lax.axis_size("cache")
    share = group_rows // owners
    rows = group_rows // RING
    chunks = steps * RING
    blocks = cols // BLK
    half, part = rows // 2, rows // RING // 2
    pieces = cols // 2 // BLK
    split = width // 3 * 2
    flows = steps + 1
    sends = 2 * steps + 3 * flows + 2 + pieces
    arrivals = 2 * steps + 7 * flows + 2 * pieces + 1
    vmem = pl.BlockSpec(memory_space=pltpu.VMEM)
    smem = pl.BlockSpec(memory_space=pltpu.SMEM)
    anywhere = pl.BlockSpec(memory_space=pl.ANY)
    small = pltpu.VMEM((chunks, blocks, rows), F32)
    a, b = pl.pallas_call(
        functools.partial(kernel, split),
        out_shape=(
            jax.ShapeDtypeStruct((steps, share, width), F32),
            jax.ShapeDtypeStruct((cols, width), F32),
        ),
        in_specs=[anywhere, vmem, vmem, smem, smem, anywhere, anywhere],
        out_specs=(anywhere, anywhere),
        scratch_shapes=[
            pltpu.VMEM((steps, group_rows, width), BF16),
            pltpu.VMEM((steps, cols, width), BF16),
            pltpu.VMEM((steps, cols, width), BF16),
            pltpu.VMEM((chunks, cols, rows), F32),
            pltpu.VMEM((cols, 2 * rows), F32),
            pltpu.VMEM((cols, rows), BF16),
            pltpu.VMEM((cols, rows), BF16),
            pltpu.VMEM((2 * BLK, chunks * rows), BF16),
            pltpu.VMEM((2 * BLK, chunks * rows), BF16),
            small, small, small, small,
            pltpu.VMEM((chunks, 8, rows), jnp.int32),
            pltpu.VMEM((steps, 8, rows), F32),
            pltpu.VMEM((steps, 2, 8, rows), F32),
            pltpu.VMEM((steps, 2, 7, 8, rows), F32),
            pltpu.VMEM((steps, RING, rows, width), F32),
            pltpu.VMEM((steps, 6, half, width), F32),
            pltpu.VMEM((steps, rows, width), F32),
            pltpu.VMEM((steps, 6, part, width), F32),
            pltpu.VMEM((steps, part, width), F32),
            pltpu.VMEM((cols, width), F32),
            pltpu.VMEM((pieces, BLK, width), F32),
            pltpu.VMEM((pieces, BLK, width), F32),
            pltpu.SemaphoreType.DMA((1 + fresh.shape[0] // rows + steps,)),
            pltpu.SemaphoreType.DMA((flows + 1,)),
            pltpu.SemaphoreType.DMA((sends,)),
            pltpu.SemaphoreType.DMA((arrivals,)),
        ],
        compiler_params=pltpu.CompilerParams(
            collective_id=0, has_side_effects=True, vmem_limit_bytes=67_043_328
        ),
        name="cache_step",
    )(queries, positives, block_list, block_count, refresh_owner, cache, fresh)
    return pl.pallas_call(
        publish,
        out_shape=(jax.ShapeDtypeStruct(a.shape, F32), jax.ShapeDtypeStruct(b.shape, F32)),
        in_specs=[anywhere, anywhere],
        out_specs=(anywhere, anywhere),
        scratch_shapes=[
            pltpu.VMEM(a.shape, F32),
            pltpu.VMEM(b.shape, F32),
            pltpu.SemaphoreType.DMA((2, cols // BLK + 1)),
        ],
        name="publish",
    )(a, b)


def solution(mesh):
    return jax.shard_map(
        on_device,
        mesh=mesh,
        in_specs=(
            P(None, "batch", None),
            P(None, "batch"),
            P(None, "batch", None),
            P(None, "batch"),
            P(),
            P("cache", None),
            P("cache", None),
        ),
        out_specs=(P(None, ("batch", "cache"), None), P("cache", None)),
        check_vma=False,
    )
```
